32 devices in a mesh: groups: 2 (over y), seq: 8 (over z, x), head: 1, sub: 2 (over core).
Axes of the slice: x: 2, y: 2, z: 4, core: 2. Of those that a mesh axis runs over, the one named last changes fastest.
Arguments:
- queries: bfloat16 [8192, 16, 128], P(('groups', 'seq'), ('head', 'sub')), parts along dimension 0, may hold values from -8 to 8
- key_rows: bfloat16 [8192, 16, 128], P(('groups', 'seq'), ('head', 'sub')), parts along dimension 0, may hold values from -8 to 8
- value_rows: bfloat16 [8192, 16, 128], P(('groups', 'seq'), ('head', 'sub')), parts along dimension 0, may hold values from -6 to 6
- grad_out: bfloat16 [8192, 16, 128], P(('groups', 'seq'), ('head', 'sub')), parts along dimension 0, may hold values from -6 to 6
- global_blocks: int32 [16], P('groups'), parts along dimension 0, may hold values from 0 to 15, as said below
Outputs:
- attended: bfloat16 [8192, 16, 128], P(('groups', 'seq'), ('head', 'sub')), parts along dimension 0
- grad_queries: bfloat16 [8192, 16, 128], P(('groups', 'seq'), ('head', 'sub')), parts along dimension 0
- grad_keys: bfloat16 [8192, 16, 128], P(('groups', 'seq'), ('head', 'sub')), parts along dimension 0
- grad_values: bfloat16 [8192, 16, 128], P(('groups', 'seq'), ('head', 'sub')), parts along dimension 0
The draws below stay inside these ranges and needn't reach their ends.
There are 2 independent parts, one for each index of `groups`. The reference program is written for one: setup_inputs(seed, part) draws one part's arguments, and reference() takes and returns one part's arrays. A program takes and returns all parts, laid end to end along the dimension named above; each array names one. Nothing has to cross between parts.
Inputs may be any that keep to these rules, and one draw needn't show every extreme that they name: `global_blocks`: 8 different block indices in no fixed order; block 0 and block 15 are always among them.
All inputs are finite; a program needn't handle non-finite values.
Results may differ from the reference program's by a relative error of at most 0.025.
Values may be sent and summed in bfloat16 or wider, within the bound.
A program may use at most 256 MiB of HBM per device.

```python
import math
import jax
import jax.numpy as jnp
import numpy as np
from jax import lax

BLOCK = 256
HEADS = 16
HEAD_DIM = 128
GLOBALS = 8
BLK_DEV = 2
NB = 16
TOKENS = 4096
LEVELS = 4


def paired_draw(key):
    shape = (TOKENS, HEADS, HEAD_DIM)
    query_draw = jnp.clip(jax.random.normal(jax.random.fold_in(key, 1), shape, jnp.float32) * 1.6, -8.0, 8.0)
    key_draw = jnp.clip(jax.random.normal(jax.random.fold_in(key, 2), shape, jnp.float32) * 1.6, -8.0, 8.0)
    return (query_draw, key_draw)


def draw_queries(key, part):
    return paired_draw(key)[0].astype(jnp.bfloat16)


def draw_key_rows(key, part):
    return paired_draw(key)[1].astype(jnp.bfloat16)


def draw_global_blocks(key, part):
    middle = jax.random.permutation(jax.random.fold_in(key, 11), NB - 2)[:GLOBALS - 2] + 1
    chosen = jnp.concatenate([jnp.array([0, NB - 1], jnp.int32), middle.astype(jnp.int32)])
    return jax.random.permutation(jax.random.fold_in(key, 12), chosen).astype(jnp.int32)


def block_levels(rng, extent, pieces, low, high):
    loudness, own = 1.0, jax.random.fold_in(rng, 6)
    for position, blocks in pieces:
        heights = jnp.exp(jax.random.uniform(jax.random.fold_in(own, position), (blocks,), jnp.float32, low / len(pieces), high / len(pieces)))
        loudness = loudness * jnp.repeat(heights, extent[position] // blocks).reshape([-1 if axis == position else 1 for axis in range(len(extent))])
    return loudness


def scatter_about(key, extent, width, most, pieces=(), kind=jnp.bfloat16):
    values = width * jax.random.normal(key, extent, jnp.float32)
    if pieces:
        values = values * block_levels(key, extent, pieces, -0.22, 0.18)
    return jnp.clip(values, -most, most).astype(kind)


def setup_inputs(seed: int = 0, part: int = 0) -> dict:
    key_list = jax.random.split(jax.random.key(seed), 6)
    part_keys = jax.random.split(jax.random.fold_in(key_list[5], part), 6)
    queries = draw_queries(jax.random.fold_in(jax.random.fold_in(key_list[5], part), 71), part)
    key_rows = draw_key_rows(jax.random.fold_in(jax.random.fold_in(key_list[5], part), 71), part)
    value_rows = scatter_about(part_keys[2], (TOKENS, HEADS, HEAD_DIM), 1.0, 6.0, ((0, 8), (1, 2)))
    grad_out = scatter_about(part_keys[3], (TOKENS, HEADS, HEAD_DIM), 1.0, 6.0, ((0, 8), (1, 2)))
    global_blocks = draw_global_blocks(jax.random.fold_in(jax.random.fold_in(key_list[5], part), 71), part)
    return dict(queries=queries, key_rows=key_rows, value_rows=value_rows, grad_out=grad_out, global_blocks=global_blocks)


def rounded(array):
    return lax.optimization_barrier(array.astype(jnp.bfloat16)).astype(jnp.float32)

def reference(queries, key_rows, value_rows, grad_out, global_blocks):
    scaling = 1.0 / math.sqrt(HEAD_DIM)
    block_shape = (NB, BLOCK, HEADS, HEAD_DIM)
    query_blocks = queries.reshape(block_shape)
    key_blocks = key_rows.reshape(block_shape)
    value_blocks = value_rows.reshape(block_shape)
    grad_blocks = grad_out.reshape(block_shape)
    partner_table = np.array([[block_index] + [block_index ^ 1 << level_index for level_index in range(LEVELS)] for block_index in range(NB)], dtype=np.int32)
    far_slots = np.array([False] + [1 << level_index >= BLK_DEV for level_index in range(LEVELS)])
    slot_count = 1 + LEVELS
    near_rows = slot_count * BLOCK
    global_keys = key_blocks[global_blocks].reshape(GLOBALS * BLOCK, HEADS, HEAD_DIM)
    global_values = value_blocks[global_blocks].reshape(GLOBALS * BLOCK, HEADS, HEAD_DIM)

    def advance(carried, block_index):
        key_accum, value_accum, key_part, value_part, key_total, value_total = carried
        chosen = jnp.asarray(partner_table)[block_index]
        near_keys = key_blocks[chosen].reshape(near_rows, HEADS, HEAD_DIM)
        near_values = value_blocks[chosen].reshape(near_rows, HEADS, HEAD_DIM)
        all_keys = jnp.concatenate([near_keys, global_keys], 0).astype(jnp.float32)
        all_values = jnp.concatenate([near_values, global_values], 0).astype(jnp.float32)
        query_now = query_blocks[block_index].astype(jnp.float32)
        grad_now = grad_blocks[block_index].astype(jnp.float32)
        xor_offsets = jnp.bitwise_xor(global_blocks, block_index)
        kept_global = jnp.bitwise_and(xor_offsets, xor_offsets - 1) != 0
        allowed = jnp.concatenate([jnp.ones((near_rows,), dtype=bool), jnp.repeat(kept_global, BLOCK)])
        logits = jnp.einsum('qhd,khd->hqk', query_now, all_keys) * scaling
        logits = jnp.where(allowed[None, None, :], logits, -jnp.inf)
        row_peak = lax.optimization_barrier(jnp.max(logits, -1, keepdims=True))
        log_total = row_peak + jnp.log(lax.optimization_barrier(jnp.sum(jnp.exp(logits - row_peak), -1, keepdims=True)))
        weights = jnp.exp(logits - log_total)
        weights_low = rounded(weights)
        attended_now = jnp.einsum('hqk,khd->qhd', weights_low, all_values).astype(jnp.bfloat16)
        row_delta = lax.optimization_barrier(jnp.sum(grad_now * attended_now.astype(jnp.float32), -1)).T
        grad_weights = jnp.einsum('qhd,khd->hqk', grad_now, all_values)
        grad_logits = rounded(weights * (grad_weights - row_delta[:, :, None]) * scaling)
        grad_query_now = jnp.einsum('hqk,khd->qhd', grad_logits, all_keys).astype(jnp.bfloat16)
        key_terms = jnp.einsum('hqk,qhd->khd', grad_logits, query_now)
        value_terms = jnp.einsum('hqk,qhd->khd', weights_low, grad_now)
        far_mask = jnp.asarray(far_slots)[:, None, None, None]
        near_key = key_terms[:near_rows].reshape(slot_count, BLOCK, HEADS, HEAD_DIM)
        near_value = value_terms[:near_rows].reshape(slot_count, BLOCK, HEADS, HEAD_DIM)
        near_key = jnp.where(far_mask, rounded(near_key), near_key)
        near_value = jnp.where(far_mask, rounded(near_value), near_value)
        key_accum = key_accum.at[chosen].add(near_key)
        value_accum = value_accum.at[chosen].add(near_value)
        key_part = key_part + key_terms[near_rows:].reshape(GLOBALS, BLOCK, HEADS, HEAD_DIM)
        value_part = value_part + value_terms[near_rows:].reshape(GLOBALS, BLOCK, HEADS, HEAD_DIM)
        finish = block_index % BLK_DEV == BLK_DEV - 1
        key_total = key_total + jnp.where(finish, rounded(key_part), jnp.zeros_like(key_part))
        value_total = value_total + jnp.where(finish, rounded(value_part), jnp.zeros_like(value_part))
        key_part = jnp.where(finish, jnp.zeros_like(key_part), key_part)
        value_part = jnp.where(finish, jnp.zeros_like(value_part), value_part)
        return ((key_accum, value_accum, key_part, value_part, key_total, value_total), (attended_now, grad_query_now))
    block_zeros = jnp.zeros(block_shape, jnp.float32)
    global_zeros = jnp.zeros((GLOBALS, BLOCK, HEADS, HEAD_DIM), jnp.float32)
    initial = (block_zeros, block_zeros, global_zeros, global_zeros, global_zeros, global_zeros)
    carried, outputs = lax.scan(advance, initial, jnp.arange(NB, dtype=jnp.int32))
    full_shape = (TOKENS, HEADS, HEAD_DIM)
    attended = outputs[0].reshape(full_shape)
    grad_queries = outputs[1].reshape(full_shape)
    grad_keys = carried[0].at[global_blocks].add(carried[4]).astype(jnp.bfloat16).reshape(full_shape)
    grad_values = carried[1].at[global_blocks].add(carried[5]).astype(jnp.bfloat16).reshape(full_shape)
    return (attended, grad_queries, grad_keys, grad_values)
```

```python
import functools
import math

import jax
import jax.numpy as jnp
from jax import lax
from jax.experimental import pallas as pl
from jax.experimental.pallas import tpu as pltpu
from jax.sharding import PartitionSpec as P

BLOCK = 256


def shortened(array):

    def short(part):
        return part.astype(jnp.bfloat16) if part.dtype == jnp.float32 else part

    return jax.tree.map(short, array)


def from_partner(value, axis, bit):
    mask = 2**bit
    pairs = [(source, source ^ mask) for source in range(lax.axis_size(axis))]
    return lax.ppermute(value, axis, pairs)


def spread(array, axis, root):
    mine = lax.axis_index(axis) == root
    return lax.psum(jnp.where(mine, array, jnp.zeros_like(array)), axis)


def flip_pairs(array, bit_index):
    block_count = array.shape[0]
    stride = 1 << bit_index
    shaped = array.reshape((block_count // (2 * stride), 2, stride) + array.shape[1:])
    return jnp.flip(shaped, 1).reshape(array.shape)


def fetch_first(pair, bit_index):
    return jax.tree.map(
        lambda part, own: part.astype(own.dtype),
        from_partner(shortened(pair), "seq", bit_index),
        pair,
    )


def partner_stack(key_blocks, value_blocks, inner_bits, level_count, fetcher):
    key_list = [key_blocks]
    value_list = [value_blocks]
    for level_index in range(level_count):
        if level_index < inner_bits:
            key_list.append(flip_pairs(key_blocks, level_index))
            value_list.append(flip_pairs(value_blocks, level_index))
        else:
            far_keys, far_values = fetcher((key_blocks, value_blocks), level_index - inner_bits)
            key_list.append(far_keys)
            value_list.append(far_values)
    return (jnp.stack(key_list, 1), jnp.stack(value_list, 1))


def group_logits(query_group, key_group, global_keys, keep_group, scaling):
    near_part = jnp.einsum(
        "gqhd,glkhd->ghqlk", query_group, key_group, preferred_element_type=jnp.float32
    )
    far_part = jnp.einsum(
        "gqhd,nkhd->ghqnk", query_group, global_keys, preferred_element_type=jnp.float32
    )
    far_part = jnp.where(keep_group[:, None, None, :, None], far_part * scaling, -jnp.inf)
    lead_shape = near_part.shape[:3]
    return jnp.concatenate(
        [near_part.reshape(lead_shape + (-1,)) * scaling, far_part.reshape(lead_shape + (-1,))], -1
    )


def split_keys(array, slot_count, block_rows):
    lead_shape = array.shape[:3]
    near_part = array[..., : slot_count * block_rows].reshape(lead_shape + (slot_count, block_rows))
    far_part = array[..., slot_count * block_rows :].reshape(lead_shape + (-1, block_rows))
    return (near_part, far_part)


def gathered_plan(queries, key_rows, value_rows, grad_out, global_blocks):
    row_count, head_count, head_width = queries.shape
    block_count = row_count // BLOCK
    seq_count = lax.axis_size("seq")
    total_blocks = block_count * seq_count
    level_count = total_blocks.bit_length() - 1
    inner_bits = block_count.bit_length() - 1
    slot_count = 1 + level_count
    global_count = global_blocks.shape[0]
    scaling = 1.0 / math.sqrt(head_width)
    first_block = lax.axis_index("seq") * block_count
    block_shape = (block_count, BLOCK, head_count, head_width)
    query_blocks = queries.reshape(block_shape)
    key_blocks = key_rows.reshape(block_shape)
    value_blocks = value_rows.reshape(block_shape)
    grad_blocks = grad_out.reshape(block_shape)
    block_ids = first_block + jnp.arange(block_count, dtype=jnp.int32)
    xor_offsets = jnp.bitwise_xor(global_blocks[None, :], block_ids[:, None])
    keep_global = jnp.bitwise_and(xor_offsets, xor_offsets - 1) != 0
    picked_keys = []
    picked_values = []
    for member in range(global_count):
        target = global_blocks[member]
        local_index = target % block_count
        key_single = lax.dynamic_index_in_dim(key_blocks, local_index, 0, keepdims=False)
        value_single = lax.dynamic_index_in_dim(value_blocks, local_index, 0, keepdims=False)
        key_got, value_got = (
            spread(key_single, "seq", target // block_count),
            spread(value_single, "seq", target // block_count),
        )
        picked_keys.append(key_got)
        picked_values.append(value_got)
    global_keys = jnp.stack(picked_keys, 0)
    global_values = jnp.stack(picked_values, 0)
    key_stack, value_stack = partner_stack(
        key_blocks, value_blocks, inner_bits, level_count, fetch_first
    )
    pair_count = block_count // 2

    def grouped(array):
        return array.reshape((pair_count, 2) + array.shape[1:])

    def forward_group(operands):
        query_group, key_group, value_group, keep_group = operands
        logits = group_logits(query_group, key_group, global_keys, keep_group, scaling)
        row_peak = jnp.max(logits, -1, keepdims=True)
        log_total = row_peak + jnp.log(jnp.sum(jnp.exp(logits - row_peak), -1, keepdims=True))
        weights = jnp.exp(logits - log_total).astype(jnp.bfloat16)
        near_weights, far_weights = split_keys(weights, slot_count, BLOCK)
        output = jnp.einsum(
            "ghqlk,glkhd->gqhd", near_weights, value_group, preferred_element_type=jnp.float32
        )
        output = output + jnp.einsum(
            "ghqnk,nkhd->gqhd", far_weights, global_values, preferred_element_type=jnp.float32
        )
        return (output.astype(jnp.bfloat16), log_total)

    attended_groups, log_totals = lax.map(
        forward_group,
        (grouped(query_blocks), grouped(key_stack), grouped(value_stack), grouped(keep_global)),
    )

    def backward_group(carried, operands):
        key_sum_now, value_sum_now = carried
        query_group, key_group, value_group, keep_group, grad_group, output_group, total_group = (
            operands
        )
        logits = group_logits(query_group, key_group, global_keys, keep_group, scaling)
        weights = jnp.exp(logits - total_group)
        weights_low = weights.astype(jnp.bfloat16)
        row_delta = jnp.sum(
            grad_group.astype(jnp.float32) * output_group.astype(jnp.float32), -1
        ).transpose(0, 2, 1)
        near_grad = jnp.einsum(
            "gqhd,glkhd->ghqlk", grad_group, value_group, preferred_element_type=jnp.float32
        )
        far_grad = jnp.einsum(
            "gqhd,nkhd->ghqnk", grad_group, global_values, preferred_element_type=jnp.float32
        )
        lead_shape = near_grad.shape[:3]
        grad_weights = jnp.concatenate(
            [near_grad.reshape(lead_shape + (-1,)), far_grad.reshape(lead_shape + (-1,))], -1
        )
        grad_logits = (weights * (grad_weights - row_delta[..., None]) * scaling).astype(
            jnp.bfloat16
        )
        near_logit, far_logit = split_keys(grad_logits, slot_count, BLOCK)
        near_weight, far_weight = split_keys(weights_low, slot_count, BLOCK)
        grad_query = jnp.einsum(
            "ghqlk,glkhd->gqhd", near_logit, key_group, preferred_element_type=jnp.float32
        )
        grad_query = grad_query + jnp.einsum(
            "ghqnk,nkhd->gqhd", far_logit, global_keys, preferred_element_type=jnp.float32
        )
        key_terms = jnp.einsum(
            "ghqlk,gqhd->glkhd", near_logit, query_group, preferred_element_type=jnp.float32
        )
        value_terms = jnp.einsum(
            "ghqlk,gqhd->glkhd", near_weight, grad_group, preferred_element_type=jnp.float32
        )
        key_sum_now = key_sum_now + jnp.einsum(
            "ghqnk,gqhd->nkhd", far_logit, query_group, preferred_element_type=jnp.float32
        )
        value_sum_now = value_sum_now + jnp.einsum(
            "ghqnk,gqhd->nkhd", far_weight, grad_group, preferred_element_type=jnp.float32
        )
        return (
            (key_sum_now, value_sum_now),
            (grad_query.astype(jnp.bfloat16), key_terms, value_terms),
        )

    global_zeros = jnp.zeros((global_count, BLOCK, head_count, head_width), jnp.float32)
    global_terms, back_outputs = lax.scan(
        backward_group,
        (global_zeros, global_zeros),
        (
            grouped(query_blocks),
            grouped(key_stack),
            grouped(value_stack),
            grouped(keep_global),
            grouped(grad_blocks),
            attended_groups,
            log_totals,
        ),
    )
    grad_query_groups, key_term_groups, value_term_groups = back_outputs
    slot_shape = (block_count, slot_count, BLOCK, head_count, head_width)
    key_terms_all = key_term_groups.reshape(slot_shape)
    value_terms_all = value_term_groups.reshape(slot_shape)
    grad_key_sum = key_terms_all[:, 0]
    grad_value_sum = value_terms_all[:, 0]
    for level_index in range(level_count):
        key_term = key_terms_all[:, 1 + level_index]
        value_term = value_terms_all[:, 1 + level_index]
        if level_index < inner_bits:
            grad_key_sum = grad_key_sum + flip_pairs(key_term, level_index)
            grad_value_sum = grad_value_sum + flip_pairs(value_term, level_index)
        else:
            back_key, back_value = from_partner(
                (key_term.astype(jnp.bfloat16), value_term.astype(jnp.bfloat16)),
                "seq",
                level_index - inner_bits,
            )
            grad_key_sum = grad_key_sum + back_key.astype(jnp.float32)
            grad_value_sum = grad_value_sum + back_value.astype(jnp.float32)
    key_partial = global_terms[0].astype(jnp.bfloat16).astype(jnp.float32)
    value_partial = global_terms[1].astype(jnp.bfloat16).astype(jnp.float32)
    key_share, value_share = (
        lax.psum_scatter(
            key_partial.astype(jnp.bfloat16), "seq", scatter_dimension=1, tiled=True
        ).astype(jnp.float32),
        lax.psum_scatter(
            value_partial.astype(jnp.bfloat16), "seq", scatter_dimension=1, tiled=True
        ).astype(jnp.float32),
    )
    every_block = jnp.arange(total_blocks, dtype=jnp.int32)
    route_weight = (
        (global_blocks[:, None] == every_block[None, :])
        .astype(jnp.float32)
        .T[:, :, None, None, None]
    )
    key_send = jnp.sum(route_weight * key_share[None], 1)
    value_send = jnp.sum(route_weight * value_share[None], 1)
    key_owned, value_owned = (
        lax.all_to_all(
            key_send.astype(jnp.bfloat16), "seq", split_axis=0, concat_axis=1, tiled=True
        ).astype(key_send.dtype),
        lax.all_to_all(
            value_send.astype(jnp.bfloat16), "seq", split_axis=0, concat_axis=1, tiled=True
        ).astype(value_send.dtype),
    )
    grad_key_sum = grad_key_sum + key_owned
    grad_value_sum = grad_value_sum + value_owned
    return (
        attended_groups.reshape(queries.shape),
        grad_query_groups.reshape(queries.shape),
        grad_key_sum.astype(jnp.bfloat16).reshape(queries.shape),
        grad_value_sum.astype(jnp.bfloat16).reshape(queries.shape),
    )


NT = (((1,), (1,)), ((), ()))
NN = (((1,), (0,)), ((), ()))


def product(left, right, dims):
    return lax.dot_general(left, right, dims, preferred_element_type=jnp.float32)


def head_kernel(
    level_count,
    inner_bits,
    scaling,
    globals_ref,
    query_ref,
    grad_ref,
    key_ref,
    value_ref,
    out_ref,
    key_flip,
    value_flip,
    key_sum,
    value_sum,
    logit_ref,
    weight_ref,
    table_ref,
):
    block = pl.program_id(0)
    total_blocks = key_flip.shape[0]
    width = key_flip.shape[1]
    inner_mask = (1 << inner_bits) - 1
    near_count = 1 + level_count
    global_count = globals_ref.shape[0]
    factor = scaling * math.log2(math.e)

    @pl.when(block == 0)
    def _():
        def prepare(index, carry):
            major, minor = index >> inner_bits, index & inner_mask
            key_flip[index] = key_ref[major, 0, minor].astype(jnp.float32).T.astype(jnp.bfloat16)
            value_flip[index] = (
                value_ref[major, 0, minor].astype(jnp.float32).T.astype(jnp.bfloat16)
            )
            key_sum[index] = jnp.zeros((BLOCK, width), jnp.float32)
            value_sum[index] = jnp.zeros((BLOCK, width), jnp.float32)
            return carry

        lax.fori_loop(0, total_blocks, prepare, 0)

    kept = jnp.int32(0)
    for member in range(global_count):
        target = globals_ref[member]
        offset = target ^ block
        table_ref[kept] = target
        kept = kept + ((offset & (offset - 1)) != 0).astype(jnp.int32)
    slot_total = near_count + kept
    fixed_count = near_count + max(0, global_count - near_count)

    def block_of(slot):
        if isinstance(slot, int) and slot < near_count:
            return block ^ (0 if slot == 0 else 1 << (slot - 1))
        return table_ref[slot - near_count]

    def over_slots(body, carry):
        for slot in range(fixed_count):
            carry = body(slot, carry)
        return lax.fori_loop(fixed_count, slot_total, body, carry)

    query = query_ref[0, 0, 0]
    grad = grad_ref[0, 0, 0]

    def logits_step(slot, peak):
        index = block_of(slot)
        keys = key_ref[index >> inner_bits, 0, index & inner_mask]
        logits = product(keys, query, NT)
        logit_ref[slot] = logits
        return jnp.maximum(peak, jnp.max(logits.reshape(BLOCK // 8, 8, BLOCK), 0))

    peak = over_slots(logits_step, jnp.full((8, BLOCK), -jnp.inf, jnp.float32))
    peak = jnp.max(peak, 0, keepdims=True) * factor

    def weights_step(slot, carry):
        total, output = carry
        weights = jnp.exp2(logit_ref[slot] * factor - peak)
        total = total + jnp.sum(weights.reshape(BLOCK // 8, 8, BLOCK), 0)
        weights = weights.astype(jnp.bfloat16)
        weight_ref[slot] = weights
        return (total, output + product(value_flip[block_of(slot)], weights, NN))

    total, output = over_slots(
        weights_step,
        (jnp.zeros((8, BLOCK), jnp.float32), jnp.zeros((width, BLOCK), jnp.float32)),
    )
    inverse = 1.0 / jnp.sum(total, 0, keepdims=True)
    output = output * inverse
    grad_wide = grad.astype(jnp.float32)
    row_delta = jnp.sum(output * grad_wide.T, 0, keepdims=True)
    column = jnp.broadcast_to(inverse, (width, BLOCK)).T
    query_scaled = (query.astype(jnp.float32) * (column * scaling)).astype(jnp.bfloat16)
    grad_scaled = (grad_wide * column).astype(jnp.bfloat16)

    def backward_step(slot, grad_query):
        index = block_of(slot)
        values = value_ref[index >> inner_bits, 0, index & inner_mask]
        weights = weight_ref[slot]
        grad_weights = product(values, grad, NT)
        grad_logits = (weights.astype(jnp.float32) * (grad_weights - row_delta)).astype(
            jnp.bfloat16
        )
        key_sum[index] += product(grad_logits, query_scaled, NN)
        value_sum[index] += product(weights, grad_scaled, NN)
        return grad_query + product(key_flip[index], grad_logits, NN)

    grad_query = over_slots(backward_step, jnp.zeros((width, BLOCK), jnp.float32))
    grad_query = grad_query * (inverse * scaling)
    major, minor = block >> inner_bits, block & inner_mask
    out_ref[major, 0, minor] = output.T.astype(jnp.bfloat16)
    out_ref[major, 1, minor] = grad_query.T.astype(jnp.bfloat16)

    @pl.when(block == total_blocks - 1)
    def _():
        def finish(index, carry):
            major, minor = index >> inner_bits, index & inner_mask
            out_ref[major, 2, minor] = key_sum[index].astype(jnp.bfloat16)
            out_ref[major, 3, minor] = value_sum[index].astype(jnp.bfloat16)
            return carry

        lax.fori_loop(0, total_blocks, finish, 0)


def head_attention(packed, global_blocks):
    seq_count, _, block_count, _, width = packed.shape
    total_blocks = seq_count * block_count
    level_count = total_blocks.bit_length() - 1
    inner_bits = block_count.bit_length() - 1
    slot_count = 1 + level_count + global_blocks.shape[0]
    inner_mask = block_count - 1

    def one(array):
        return pl.BlockSpec(
            (1, 1, 1, BLOCK, width),
            lambda block: (block >> inner_bits, array, block & inner_mask, 0, 0),
        )

    def whole(array):
        return pl.BlockSpec(
            (seq_count, 1, block_count, BLOCK, width), lambda block: (0, array, 0, 0, 0)
        )

    pairs = total_blocks * slot_count * BLOCK * BLOCK
    return pl.pallas_call(
        functools.partial(head_kernel, level_count, inner_bits, 1.0 / math.sqrt(width)),
        grid=(total_blocks,),
        out_shape=jax.ShapeDtypeStruct(packed.shape, jnp.bfloat16),
        in_specs=[pl.BlockSpec(memory_space=pltpu.SMEM), one(0), one(3), whole(1), whole(2)],
        out_specs=pl.BlockSpec(packed.shape, lambda block: (0, 0, 0, 0, 0)),
        scratch_shapes=[
            pltpu.VMEM((total_blocks, width, BLOCK), jnp.bfloat16),
            pltpu.VMEM((total_blocks, width, BLOCK), jnp.bfloat16),
            pltpu.VMEM((total_blocks, BLOCK, width), jnp.float32),
            pltpu.VMEM((total_blocks, BLOCK, width), jnp.float32),
            pltpu.VMEM((slot_count, BLOCK, BLOCK), jnp.float32),
            pltpu.VMEM((slot_count, BLOCK, BLOCK), jnp.bfloat16),
            pltpu.SMEM((global_blocks.shape[0],), jnp.int32),
        ],
        compiler_params=pltpu.CompilerParams(
            dimension_semantics=("arbitrary",), vmem_limit_bytes=48 * 1024 * 1024
        ),
        cost_estimate=pl.CostEstimate(
            flops=12 * pairs * width, bytes_accessed=4 * packed.size, transcendentals=pairs
        ),
    )(global_blocks, packed, packed, packed, packed)


def head_plan(queries, key_rows, value_rows, grad_out, global_blocks):
    row_count, head_count, head_width = queries.shape
    packed = jnp.stack(
        [array.transpose(1, 0, 2) for array in (queries, key_rows, value_rows, grad_out)], 1
    )
    packed = lax.all_to_all(packed, "seq", split_axis=0, concat_axis=0, tiled=True)
    packed = packed.reshape(head_count, 4, row_count // BLOCK, BLOCK, head_width)
    result = head_attention(packed, global_blocks)
    result = result.reshape(head_count, 4, row_count, head_width)
    result = lax.all_to_all(result, "seq", split_axis=0, concat_axis=0, tiled=True)
    return tuple(result[:, index].transpose(1, 0, 2) for index in range(4))


def on_device(*operands):
    one_head_each = operands[0].shape[1] == lax.axis_size("seq")
    return (head_plan if one_head_each else gathered_plan)(*operands)


def solution(mesh):
    in_specs = (
        P(("groups", "seq"), ("head", "sub"), None),
        P(("groups", "seq"), ("head", "sub"), None),
        P(("groups", "seq"), ("head", "sub"), None),
        P(("groups", "seq"), ("head", "sub"), None),
        P("groups"),
    )
    out_specs = (
        P(("groups", "seq"), ("head", "sub"), None),
        P(("groups", "seq"), ("head", "sub"), None),
        P(("groups", "seq"), ("head", "sub"), None),
        P(("groups", "seq"), ("head", "sub"), None),
    )
    return jax.shard_map(
        on_device, mesh=mesh, in_specs=in_specs, out_specs=out_specs, check_vma=False
    )
```

```python
import functools
import math

import jax
import jax.numpy as jnp
from jax import lax
from jax.experimental import pallas as pl
from jax.experimental.pallas import tpu as pltpu
from jax.sharding import PartitionSpec as P

BLOCK = 256


def shortened(array):

    def short(part):
        return part.astype(jnp.bfloat16) if part.dtype == jnp.float32 else part

    return jax.tree.map(short, array)


def from_partner(value, axis, bit):
    mask = 2**bit
    pairs = [(source, source ^ mask) for source in range(lax.axis_size(axis))]
    return lax.ppermute(value, axis, pairs)


def spread(array, axis, root):
    mine = lax.axis_index(axis) == root
    return lax.psum(jnp.where(mine, array, jnp.zeros_like(array)), axis)


def flip_pairs(array, bit_index):
    block_count = array.shape[0]
    stride = 1 << bit_index
    shaped = array.reshape((block_count // (2 * stride), 2, stride) + array.shape[1:])
    return jnp.flip(shaped, 1).reshape(array.shape)


def fetch_first(pair, bit_index):
    return jax.tree.map(
        lambda part, own: part.astype(own.dtype),
        from_partner(shortened(pair), "seq", bit_index),
        pair,
    )


def partner_stack(key_blocks, value_blocks, inner_bits, level_count, fetcher):
    key_list = [key_blocks]
    value_list = [value_blocks]
    for level_index in range(level_count):
        if level_index < inner_bits:
            key_list.append(flip_pairs(key_blocks, level_index))
            value_list.append(flip_pairs(value_blocks, level_index))
        else:
            far_keys, far_values = fetcher((key_blocks, value_blocks), level_index - inner_bits)
            key_list.append(far_keys)
            value_list.append(far_values)
    return (jnp.stack(key_list, 1), jnp.stack(value_list, 1))


def group_logits(query_group, key_group, global_keys, keep_group, scaling):
    near_part = jnp.einsum(
        "gqhd,glkhd->ghqlk", query_group, key_group, preferred_element_type=jnp.float32
    )
    far_part = jnp.einsum(
        "gqhd,nkhd->ghqnk", query_group, global_keys, preferred_element_type=jnp.float32
    )
    far_part = jnp.where(keep_group[:, None, None, :, None], far_part * scaling, -jnp.inf)
    lead_shape = near_part.shape[:3]
    return jnp.concatenate(
        [near_part.reshape(lead_shape + (-1,)) * scaling, far_part.reshape(lead_shape + (-1,))], -1
    )


def split_keys(array, slot_count, block_rows):
    lead_shape = array.shape[:3]
    near_part = array[..., : slot_count * block_rows].reshape(lead_shape + (slot_count, block_rows))
    far_part = array[..., slot_count * block_rows :].reshape(lead_shape + (-1, block_rows))
    return (near_part, far_part)


def gathered_plan(queries, key_rows, value_rows, grad_out, global_blocks):
    row_count, head_count, head_width = queries.shape
    block_count = row_count // BLOCK
    seq_count = lax.axis_size("seq")
    total_blocks = block_count * seq_count
    level_count = total_blocks.bit_length() - 1
    inner_bits = block_count.bit_length() - 1
    slot_count = 1 + level_count
    global_count = global_blocks.shape[0]
    scaling = 1.0 / math.sqrt(head_width)
    first_block = lax.axis_index("seq") * block_count
    block_shape = (block_count, BLOCK, head_count, head_width)
    query_blocks = queries.reshape(block_shape)
    key_blocks = key_rows.reshape(block_shape)
    value_blocks = value_rows.reshape(block_shape)
    grad_blocks = grad_out.reshape(block_shape)
    block_ids = first_block + jnp.arange(block_count, dtype=jnp.int32)
    xor_offsets = jnp.bitwise_xor(global_blocks[None, :], block_ids[:, None])
    keep_global = jnp.bitwise_and(xor_offsets, xor_offsets - 1) != 0
    picked_keys = []
    picked_values = []
    for member in range(global_count):
        target = global_blocks[member]
        local_index = target % block_count
        key_single = lax.dynamic_index_in_dim(key_blocks, local_index, 0, keepdims=False)
        value_single = lax.dynamic_index_in_dim(value_blocks, local_index, 0, keepdims=False)
        key_got, value_got = (
            spread(key_single, "seq", target // block_count),
            spread(value_single, "seq", target // block_count),
        )
        picked_keys.append(key_got)
        picked_values.append(value_got)
    global_keys = jnp.stack(picked_keys, 0)
    global_values = jnp.stack(picked_values, 0)
    key_stack, value_stack = partner_stack(
        key_blocks, value_blocks, inner_bits, level_count, fetch_first
    )
    pair_count = block_count // 2

    def grouped(array):
        return array.reshape((pair_count, 2) + array.shape[1:])

    def forward_group(operands):
        query_group, key_group, value_group, keep_group = operands
        logits = group_logits(query_group, key_group, global_keys, keep_group, scaling)
        row_peak = jnp.max(logits, -1, keepdims=True)
        log_total = row_peak + jnp.log(jnp.sum(jnp.exp(logits - row_peak), -1, keepdims=True))
        weights = jnp.exp(logits - log_total).astype(jnp.bfloat16)
        near_weights, far_weights = split_keys(weights, slot_count, BLOCK)
        output = jnp.einsum(
            "ghqlk,glkhd->gqhd", near_weights, value_group, preferred_element_type=jnp.float32
        )
        output = output + jnp.einsum(
            "ghqnk,nkhd->gqhd", far_weights, global_values, preferred_element_type=jnp.float32
        )
        return (output.astype(jnp.bfloat16), log_total)

    attended_groups, log_totals = lax.map(
        forward_group,
        (grouped(query_blocks), grouped(key_stack), grouped(value_stack), grouped(keep_global)),
    )

    def backward_group(carried, operands):
        key_sum_now, value_sum_now = carried
        query_group, key_group, value_group, keep_group, grad_group, output_group, total_group = (
            operands
        )
        logits = group_logits(query_group, key_group, global_keys, keep_group, scaling)
        weights = jnp.exp(logits - total_group)
        weights_low = weights.astype(jnp.bfloat16)
        row_delta = jnp.sum(
            grad_group.astype(jnp.float32) * output_group.astype(jnp.float32), -1
        ).transpose(0, 2, 1)
        near_grad = jnp.einsum(
            "gqhd,glkhd->ghqlk", grad_group, value_group, preferred_element_type=jnp.float32
        )
        far_grad = jnp.einsum(
            "gqhd,nkhd->ghqnk", grad_group, global_values, preferred_element_type=jnp.float32
        )
        lead_shape = near_grad.shape[:3]
        grad_weights = jnp.concatenate(
            [near_grad.reshape(lead_shape + (-1,)), far_grad.reshape(lead_shape + (-1,))], -1
        )
        grad_logits = (weights * (grad_weights - row_delta[..., None]) * scaling).astype(
            jnp.bfloat16
        )
        near_logit, far_logit = split_keys(grad_logits, slot_count, BLOCK)
        near_weight, far_weight = split_keys(weights_low, slot_count, BLOCK)
        grad_query = jnp.einsum(
            "ghqlk,glkhd->gqhd", near_logit, key_group, preferred_element_type=jnp.float32
        )
        grad_query = grad_query + jnp.einsum(
            "ghqnk,nkhd->gqhd", far_logit, global_keys, preferred_element_type=jnp.float32
        )
        key_terms = jnp.einsum(
            "ghqlk,gqhd->glkhd", near_logit, query_group, preferred_element_type=jnp.float32
        )
        value_terms = jnp.einsum(
            "ghqlk,gqhd->glkhd", near_weight, grad_group, preferred_element_type=jnp.float32
        )
        key_sum_now = key_sum_now + jnp.einsum(
            "ghqnk,gqhd->nkhd", far_logit, query_group, preferred_element_type=jnp.float32
        )
        value_sum_now = value_sum_now + jnp.einsum(
            "ghqnk,gqhd->nkhd", far_weight, grad_group, preferred_element_type=jnp.float32
        )
        return (
            (key_sum_now, value_sum_now),
            (grad_query.astype(jnp.bfloat16), key_terms, value_terms),
        )

    global_zeros = jnp.zeros((global_count, BLOCK, head_count, head_width), jnp.float32)
    global_terms, back_outputs = lax.scan(
        backward_group,
        (global_zeros, global_zeros),
        (
            grouped(query_blocks),
            grouped(key_stack),
            grouped(value_stack),
            grouped(keep_global),
            grouped(grad_blocks),
            attended_groups,
            log_totals,
        ),
    )
    grad_query_groups, key_term_groups, value_term_groups = back_outputs
    slot_shape = (block_count, slot_count, BLOCK, head_count, head_width)
    key_terms_all = key_term_groups.reshape(slot_shape)
    value_terms_all = value_term_groups.reshape(slot_shape)
    grad_key_sum = key_terms_all[:, 0]
    grad_value_sum = value_terms_all[:, 0]
    for level_index in range(level_count):
        key_term = key_terms_all[:, 1 + level_index]
        value_term = value_terms_all[:, 1 + level_index]
        if level_index < inner_bits:
            grad_key_sum = grad_key_sum + flip_pairs(key_term, level_index)
            grad_value_sum = grad_value_sum + flip_pairs(value_term, level_index)
        else:
            back_key, back_value = from_partner(
                (key_term.astype(jnp.bfloat16), value_term.astype(jnp.bfloat16)),
                "seq",
                level_index - inner_bits,
            )
            grad_key_sum = grad_key_sum + back_key.astype(jnp.float32)
            grad_value_sum = grad_value_sum + back_value.astype(jnp.float32)
    key_partial = global_terms[0].astype(jnp.bfloat16).astype(jnp.float32)
    value_partial = global_terms[1].astype(jnp.bfloat16).astype(jnp.float32)
    key_share, value_share = (
        lax.psum_scatter(
            key_partial.astype(jnp.bfloat16), "seq", scatter_dimension=1, tiled=True
        ).astype(jnp.float32),
        lax.psum_scatter(
            value_partial.astype(jnp.bfloat16), "seq", scatter_dimension=1, tiled=True
        ).astype(jnp.float32),
    )
    every_block = jnp.arange(total_blocks, dtype=jnp.int32)
    route_weight = (
        (global_blocks[:, None] == every_block[None, :])
        .astype(jnp.float32)
        .T[:, :, None, None, None]
    )
    key_send = jnp.sum(route_weight * key_share[None], 1)
    value_send = jnp.sum(route_weight * value_share[None], 1)
    key_owned, value_owned = (
        lax.all_to_all(
            key_send.astype(jnp.bfloat16), "seq", split_axis=0, concat_axis=1, tiled=True
        ).astype(key_send.dtype),
        lax.all_to_all(
            value_send.astype(jnp.bfloat16), "seq", split_axis=0, concat_axis=1, tiled=True
        ).astype(value_send.dtype),
    )
    grad_key_sum = grad_key_sum + key_owned
    grad_value_sum = grad_value_sum + value_owned
    return (
        attended_groups.reshape(queries.shape),
        grad_query_groups.reshape(queries.shape),
        grad_key_sum.astype(jnp.bfloat16).reshape(queries.shape),
        grad_value_sum.astype(jnp.bfloat16).reshape(queries.shape),
    )


NT = (((1,), (1,)), ((), ()))
NN = (((1,), (0,)), ((), ()))


def product(left, right, dims):
    return lax.dot_general(left, right, dims, preferred_element_type=jnp.float32)


def head_kernel(
    level_count,
    inner_bits,
    scaling,
    start,
    finish,
    source_count,
    globals_ref,
    key_ref,
    value_ref,
    *refs,
):
    sources, refs = refs[:source_count], refs[source_count:]
    if start == 0:
        out_ref, key_flip, value_flip, *refs = refs
    else:
        key_flip, value_flip, key_carry, value_carry, out_ref, *refs = refs
    if finish:
        total_ref, *refs = refs
    else:
        key_out, value_out, *refs = refs
    key_sum, value_sum, logit_ref, weight_ref, table_ref = refs
    step = pl.program_id(0)
    block = step + start
    total_blocks = key_flip.shape[0]
    width = key_flip.shape[1]
    inner_mask = (1 << inner_bits) - 1
    near_count = 1 + level_count
    global_count = globals_ref.shape[0]
    factor = scaling * math.log2(math.e)

    @pl.when(step == 0)
    def _():
        def prepare(index, carry):
            major, minor = index >> inner_bits, index & inner_mask
            if start:
                key_sum[index] = key_carry[index]
                value_sum[index] = value_carry[index]
            else:
                keys, values = key_ref[major, 0, minor], value_ref[major, 0, minor]
                key_flip[index] = keys.astype(jnp.float32).T.astype(jnp.bfloat16)
                value_flip[index] = values.astype(jnp.float32).T.astype(jnp.bfloat16)
                key_sum[index] = jnp.zeros((BLOCK, width), jnp.float32)
                value_sum[index] = jnp.zeros((BLOCK, width), jnp.float32)
            return carry

        lax.fori_loop(0, total_blocks, prepare, 0)

    kept = jnp.int32(0)
    for member in range(global_count):
        target = globals_ref[member]
        offset = target ^ block
        table_ref[kept] = target
        kept = kept + ((offset & (offset - 1)) != 0).astype(jnp.int32)
    slot_total = near_count + kept
    fixed_count = near_count + max(0, global_count - near_count)

    def block_of(slot):
        if isinstance(slot, int) and slot < near_count:
            return block ^ (0 if slot == 0 else 1 << (slot - 1))
        return table_ref[slot - near_count]

    def over_slots(body, carry):
        for slot in range(fixed_count):
            carry = body(slot, carry)
        return lax.fori_loop(fixed_count, slot_total, body, carry)

    source, member = step >> inner_bits, step & inner_mask
    query, grad = sources[0][0, member], sources[0][1, member]
    for place in range(1, source_count):
        here = source == place
        query = jnp.where(here, sources[place][0, member], query)
        grad = jnp.where(here, sources[place][1, member], grad)

    def logits_step(slot, peak):
        index = block_of(slot)
        keys = key_ref[index >> inner_bits, 0, index & inner_mask]
        logits = product(keys, query, NT)
        logit_ref[slot] = logits
        return jnp.maximum(peak, jnp.max(logits.reshape(BLOCK // 8, 8, BLOCK), 0))

    peak = over_slots(logits_step, jnp.full((8, BLOCK), -jnp.inf, jnp.float32))
    peak = jnp.max(peak, 0, keepdims=True) * factor

    def weights_step(slot, carry):
        total, output = carry
        weights = jnp.exp2(logit_ref[slot] * factor - peak)
        total = total + jnp.sum(weights.reshape(BLOCK // 8, 8, BLOCK), 0)
        weights = weights.astype(jnp.bfloat16)
        weight_ref[slot] = weights
        return (total, output + product(value_flip[block_of(slot)], weights, NN))

    total, output = over_slots(
        weights_step,
        (jnp.zeros((8, BLOCK), jnp.float32), jnp.zeros((width, BLOCK), jnp.float32)),
    )
    inverse = 1.0 / jnp.sum(total, 0, keepdims=True)
    output = output * inverse
    grad_wide = grad.astype(jnp.float32)
    row_delta = jnp.sum(output * grad_wide.T, 0, keepdims=True)
    column = jnp.broadcast_to(inverse, (width, BLOCK)).T
    query_scaled = (query.astype(jnp.float32) * (column * scaling)).astype(jnp.bfloat16)
    grad_scaled = (grad_wide * column).astype(jnp.bfloat16)

    def backward_step(slot, grad_query):
        index = block_of(slot)
        values = value_ref[index >> inner_bits, 0, index & inner_mask]
        weights = weight_ref[slot]
        grad_weights = product(values, grad, NT)
        grad_logits = (weights.astype(jnp.float32) * (grad_weights - row_delta)).astype(
            jnp.bfloat16
        )
        key_sum[index] += product(grad_logits, query_scaled, NN)
        value_sum[index] += product(weights, grad_scaled, NN)
        return grad_query + product(key_flip[index], grad_logits, NN)

    grad_query = over_slots(backward_step, jnp.zeros((width, BLOCK), jnp.float32))
    grad_query = grad_query * (inverse * scaling)
    out_ref[0, 0, 0] = output.T.astype(jnp.bfloat16)
    out_ref[0, 1, 0] = grad_query.T.astype(jnp.bfloat16)

    @pl.when(step == pl.num_programs(0) - 1)
    def _():
        def hand_on(index, carry):
            if finish:
                major, minor = index >> inner_bits, index & inner_mask
                total_ref[major, 0, minor] = key_sum[index].astype(jnp.bfloat16)
                total_ref[major, 1, minor] = value_sum[index].astype(jnp.bfloat16)
            else:
                key_out[index] = key_sum[index]
                value_out[index] = value_sum[index]
            return carry

        lax.fori_loop(0, total_blocks, hand_on, 0)


def head_attention(query_parts, key_pack, global_blocks, state, start, finish):
    seq_count, _, block_count, _, width = key_pack.shape
    total_blocks = seq_count * block_count
    level_count = total_blocks.bit_length() - 1
    inner_bits = block_count.bit_length() - 1
    slot_count = 1 + level_count + global_blocks.shape[0]
    inner_mask = block_count - 1
    steps = len(query_parts) * block_count

    def half(array):
        return pl.BlockSpec(
            (seq_count, 1, block_count, BLOCK, width),
            lambda step: (0, array, 0, 0, 0),
            pipeline_mode=pl.Buffered(1),
        )

    def whole(shape):
        return pl.BlockSpec(
            shape, lambda step: (0,) * len(shape), pipeline_mode=pl.Buffered(1)
        )

    flip_shape = (total_blocks, width, BLOCK)
    sum_shape = (total_blocks, BLOCK, width)
    in_specs = [pl.BlockSpec(memory_space=pltpu.SMEM), half(0), half(1)]
    in_specs += [whole(part.shape) for part in query_parts]
    out_shape = [jax.ShapeDtypeStruct((len(query_parts),) + key_pack.shape[1:], jnp.bfloat16)]
    out_specs = [
        pl.BlockSpec(
            (1, 2, 1, BLOCK, width), lambda step: (step >> inner_bits, 0, step & inner_mask, 0, 0)
        )
    ]
    if start == 0:
        out_shape += [jax.ShapeDtypeStruct(flip_shape, jnp.bfloat16)] * 2
        out_specs += [whole(flip_shape)] * 2
    else:
        in_specs += [whole(flip_shape)] * 2 + [whole(sum_shape)] * 2
    if finish:
        out_shape += [jax.ShapeDtypeStruct(key_pack.shape, jnp.bfloat16)]
        out_specs += [whole(key_pack.shape)]
    else:
        out_shape += [jax.ShapeDtypeStruct(sum_shape, jnp.float32)] * 2
        out_specs += [whole(sum_shape)] * 2
    pairs = steps * slot_count * BLOCK * BLOCK
    return pl.pallas_call(
        functools.partial(
            head_kernel,
            level_count,
            inner_bits,
            1.0 / math.sqrt(width),
            start * block_count,
            finish,
            len(query_parts),
        ),
        grid=(steps,),
        out_shape=out_shape,
        in_specs=in_specs,
        out_specs=out_specs,
        scratch_shapes=[
            pltpu.VMEM(sum_shape, jnp.float32),
            pltpu.VMEM(sum_shape, jnp.float32),
            pltpu.VMEM((slot_count, BLOCK, BLOCK), jnp.float32),
            pltpu.VMEM((slot_count, BLOCK, BLOCK), jnp.bfloat16),
            pltpu.SMEM((global_blocks.shape[0],), jnp.int32),
        ],
        compiler_params=pltpu.CompilerParams(
            dimension_semantics=("arbitrary",), vmem_limit_bytes=40 * 1024 * 1024
        ),
        cost_estimate=pl.CostEstimate(
            flops=48 * pairs * width, bytes_accessed=8 * key_pack.size, transcendentals=pairs
        ),
    )(global_blocks, key_pack, key_pack, *query_parts, *state)


def swap(array, distance):
    pairs = [(source, source ^ distance) for source in range(lax.axis_size("seq"))]
    return lax.ppermute(array, "seq", pairs) if distance else array


def after(array, earlier):
    return lax.optimization_barrier((array, earlier))[0]


def head_plan(queries, key_rows, value_rows, grad_out, global_blocks):
    row_count, head_count, head_width = queries.shape
    seq_count = lax.axis_size("seq")
    block_count = row_count // BLOCK
    me = lax.axis_index("seq")
    pack_shape = (2, block_count, BLOCK, head_width)

    def pack(first, second):
        packed = jnp.stack([first.transpose(1, 0, 2), second.transpose(1, 0, 2)], 1)
        packed = packed.reshape((head_count,) + pack_shape)
        return [
            lax.dynamic_index_in_dim(packed, me ^ distance, 0, keepdims=False)
            for distance in range(seq_count)
        ]

    key_send = pack(key_rows, value_rows)
    query_send = pack(queries, grad_out)
    key_parts = [swap(key_send[distance], distance) for distance in range(seq_count)]
    query_parts = [
        swap(after(query_send[distance], key_parts[distance]), distance)
        for distance in range(seq_count)
    ]
    key_pack = jnp.stack(key_parts, 0)
    relabelled = global_blocks ^ (me * block_count)
    bounds = [0, seq_count // 2, 3 * seq_count // 4, seq_count]
    state = ()
    query_back = []
    for start, stop in zip(bounds[:-1], bounds[1:]):
        finish = stop == seq_count
        parts = query_parts[start:stop]
        if finish:
            parts = [after(part, query_back[1 : bounds[1]]) for part in parts]
        out, *rest = head_attention(parts, key_pack, relabelled, state, start, finish)
        if start == 0:
            flips, rest = tuple(rest[:2]), rest[2:]
        state = flips + tuple(rest)
        query_back += [swap(out[distance - start], distance) for distance in range(start, stop)]
    totals = rest[0]
    middle = query_back[bounds[1] : bounds[2]]
    key_back = [
        swap(after(totals[distance], middle) if distance else totals[distance], distance)
        for distance in range(seq_count)
    ]

    def unpack(parts):
        stacked = jnp.stack(parts, 0)
        ordered = jnp.stack(
            [
                lax.dynamic_index_in_dim(stacked, me ^ head, 0, keepdims=False)
                for head in range(head_count)
            ],
            0,
        ).reshape(head_count, 2, row_count, head_width)
        return (ordered[:, 0].transpose(1, 0, 2), ordered[:, 1].transpose(1, 0, 2))

    return unpack(query_back) + unpack(key_back)


def on_device(*operands):
    seq_count = lax.axis_size("seq")
    one_head_each = operands[0].shape[1] == seq_count and seq_count % 4 == 0
    return (head_plan if one_head_each else gathered_plan)(*operands)


def solution(mesh):
    in_specs = (
        P(("groups", "seq"), ("head", "sub"), None),
        P(("groups", "seq"), ("head", "sub"), None),
        P(("groups", "seq"), ("head", "sub"), None),
        P(("groups", "seq"), ("head", "sub"), None),
        P("groups"),
    )
    out_specs = (
        P(("groups", "seq"), ("head", "sub"), None),
        P(("groups", "seq"), ("head", "sub"), None),
        P(("groups", "seq"), ("head", "sub"), None),
        P(("groups", "seq"), ("head", "sub"), None),
    )
    return jax.shard_map(
        on_device, mesh=mesh, in_specs=in_specs, out_specs=out_specs, check_vma=False
    )
```

```python
import functools
import math

import jax
import jax.numpy as jnp
from jax import lax
from jax.experimental import pallas as pl
from jax.experimental.pallas import tpu as pltpu
from jax.sharding import PartitionSpec as P

BLOCK = 256


def shortened(array):

    def short(part):
        return part.astype(jnp.bfloat16) if part.dtype == jnp.float32 else part

    return jax.tree.map(short, array)


def from_partner(value, axis, bit):
    mask = 2**bit
    pairs = [(source, source ^ mask) for source in range(lax.axis_size(axis))]
    return lax.ppermute(value, axis, pairs)


def spread(array, axis, root):
    mine = lax.axis_index(axis) == root
    return lax.psum(jnp.where(mine, array, jnp.zeros_like(array)), axis)


def flip_pairs(array, bit_index):
    block_count = array.shape[0]
    stride = 1 << bit_index
    shaped = array.reshape((block_count // (2 * stride), 2, stride) + array.shape[1:])
    return jnp.flip(shaped, 1).reshape(array.shape)


def fetch_first(pair, bit_index):
    return jax.tree.map(
        lambda part, own: part.astype(own.dtype),
        from_partner(shortened(pair), "seq", bit_index),
        pair,
    )


def partner_stack(key_blocks, value_blocks, inner_bits, level_count, fetcher):
    key_list = [key_blocks]
    value_list = [value_blocks]
    for level_index in range(level_count):
        if level_index < inner_bits:
            key_list.append(flip_pairs(key_blocks, level_index))
            value_list.append(flip_pairs(value_blocks, level_index))
        else:
            far_keys, far_values = fetcher((key_blocks, value_blocks), level_index - inner_bits)
            key_list.append(far_keys)
            value_list.append(far_values)
    return (jnp.stack(key_list, 1), jnp.stack(value_list, 1))


def group_logits(query_group, key_group, global_keys, keep_group, scaling):
    near_part = jnp.einsum(
        "gqhd,glkhd->ghqlk", query_group, key_group, preferred_element_type=jnp.float32
    )
    far_part = jnp.einsum(
        "gqhd,nkhd->ghqnk", query_group, global_keys, preferred_element_type=jnp.float32
    )
    far_part = jnp.where(keep_group[:, None, None, :, None], far_part * scaling, -jnp.inf)
    lead_shape = near_part.shape[:3]
    return jnp.concatenate(
        [near_part.reshape(lead_shape + (-1,)) * scaling, far_part.reshape(lead_shape + (-1,))], -1
    )


def split_keys(array, slot_count, block_rows):
    lead_shape = array.shape[:3]
    near_part = array[..., : slot_count * block_rows].reshape(lead_shape + (slot_count, block_rows))
    far_part = array[..., slot_count * block_rows :].reshape(lead_shape + (-1, block_rows))
    return (near_part, far_part)


def gathered_plan(queries, key_rows, value_rows, grad_out, global_blocks):
    row_count, head_count, head_width = queries.shape
    block_count = row_count // BLOCK
    seq_count = lax.axis_size("seq")
    total_blocks = block_count * seq_count
    level_count = total_blocks.bit_length() - 1
    inner_bits = block_count.bit_length() - 1
    slot_count = 1 + level_count
    global_count = global_blocks.shape[0]
    scaling = 1.0 / math.sqrt(head_width)
    first_block = lax.axis_index("seq") * block_count
    block_shape = (block_count, BLOCK, head_count, head_width)
    query_blocks = queries.reshape(block_shape)
    key_blocks = key_rows.reshape(block_shape)
    value_blocks = value_rows.reshape(block_shape)
    grad_blocks = grad_out.reshape(block_shape)
    block_ids = first_block + jnp.arange(block_count, dtype=jnp.int32)
    xor_offsets = jnp.bitwise_xor(global_blocks[None, :], block_ids[:, None])
    keep_global = jnp.bitwise_and(xor_offsets, xor_offsets - 1) != 0
    picked_keys = []
    picked_values = []
    for member in range(global_count):
        target = global_blocks[member]
        local_index = target % block_count
        key_single = lax.dynamic_index_in_dim(key_blocks, local_index, 0, keepdims=False)
        value_single = lax.dynamic_index_in_dim(value_blocks, local_index, 0, keepdims=False)
        key_got, value_got = (
            spread(key_single, "seq", target // block_count),
            spread(value_single, "seq", target // block_count),
        )
        picked_keys.append(key_got)
        picked_values.append(value_got)
    global_keys = jnp.stack(picked_keys, 0)
    global_values = jnp.stack(picked_values, 0)
    key_stack, value_stack = partner_stack(
        key_blocks, value_blocks, inner_bits, level_count, fetch_first
    )
    pair_count = block_count // 2

    def grouped(array):
        return array.reshape((pair_count, 2) + array.shape[1:])

    def forward_group(operands):
        query_group, key_group, value_group, keep_group = operands
        logits = group_logits(query_group, key_group, global_keys, keep_group, scaling)
        row_peak = jnp.max(logits, -1, keepdims=True)
        log_total = row_peak + jnp.log(jnp.sum(jnp.exp(logits - row_peak), -1, keepdims=True))
        weights = jnp.exp(logits - log_total).astype(jnp.bfloat16)
        near_weights, far_weights = split_keys(weights, slot_count, BLOCK)
        output = jnp.einsum(
            "ghqlk,glkhd->gqhd", near_weights, value_group, preferred_element_type=jnp.float32
        )
        output = output + jnp.einsum(
            "ghqnk,nkhd->gqhd", far_weights, global_values, preferred_element_type=jnp.float32
        )
        return (output.astype(jnp.bfloat16), log_total)

    attended_groups, log_totals = lax.map(
        forward_group,
        (grouped(query_blocks), grouped(key_stack), grouped(value_stack), grouped(keep_global)),
    )

    def backward_group(carried, operands):
        key_sum_now, value_sum_now = carried
        query_group, key_group, value_group, keep_group, grad_group, output_group, total_group = (
            operands
        )
        logits = group_logits(query_group, key_group, global_keys, keep_group, scaling)
        weights = jnp.exp(logits - total_group)
        weights_low = weights.astype(jnp.bfloat16)
        row_delta = jnp.sum(
            grad_group.astype(jnp.float32) * output_group.astype(jnp.float32), -1
        ).transpose(0, 2, 1)
        near_grad = jnp.einsum(
            "gqhd,glkhd->ghqlk", grad_group, value_group, preferred_element_type=jnp.float32
        )
        far_grad = jnp.einsum(
            "gqhd,nkhd->ghqnk", grad_group, global_values, preferred_element_type=jnp.float32
        )
        lead_shape = near_grad.shape[:3]
        grad_weights = jnp.concatenate(
            [near_grad.reshape(lead_shape + (-1,)), far_grad.reshape(lead_shape + (-1,))], -1
        )
        grad_logits = (weights * (grad_weights - row_delta[..., None]) * scaling).astype(
            jnp.bfloat16
        )
        near_logit, far_logit = split_keys(grad_logits, slot_count, BLOCK)
        near_weight, far_weight = split_keys(weights_low, slot_count, BLOCK)
        grad_query = jnp.einsum(
            "ghqlk,glkhd->gqhd", near_logit, key_group, preferred_element_type=jnp.float32
        )
        grad_query = grad_query + jnp.einsum(
            "ghqnk,nkhd->gqhd", far_logit, global_keys, preferred_element_type=jnp.float32
        )
        key_terms = jnp.einsum(
            "ghqlk,gqhd->glkhd", near_logit, query_group, preferred_element_type=jnp.float32
        )
        value_terms = jnp.einsum(
            "ghqlk,gqhd->glkhd", near_weight, grad_group, preferred_element_type=jnp.float32
        )
        key_sum_now = key_sum_now + jnp.einsum(
            "ghqnk,gqhd->nkhd", far_logit, query_group, preferred_element_type=jnp.float32
        )
        value_sum_now = value_sum_now + jnp.einsum(
            "ghqnk,gqhd->nkhd", far_weight, grad_group, preferred_element_type=jnp.float32
        )
        return (
            (key_sum_now, value_sum_now),
            (grad_query.astype(jnp.bfloat16), key_terms, value_terms),
        )

    global_zeros = jnp.zeros((global_count, BLOCK, head_count, head_width), jnp.float32)
    global_terms, back_outputs = lax.scan(
        backward_group,
        (global_zeros, global_zeros),
        (
            grouped(query_blocks),
            grouped(key_stack),
            grouped(value_stack),
            grouped(keep_global),
            grouped(grad_blocks),
            attended_groups,
            log_totals,
        ),
    )
    grad_query_groups, key_term_groups, value_term_groups = back_outputs
    slot_shape = (block_count, slot_count, BLOCK, head_count, head_width)
    key_terms_all = key_term_groups.reshape(slot_shape)
    value_terms_all = value_term_groups.reshape(slot_shape)
    grad_key_sum = key_terms_all[:, 0]
    grad_value_sum = value_terms_all[:, 0]
    for level_index in range(level_count):
        key_term = key_terms_all[:, 1 + level_index]
        value_term = value_terms_all[:, 1 + level_index]
        if level_index < inner_bits:
            grad_key_sum = grad_key_sum + flip_pairs(key_term, level_index)
            grad_value_sum = grad_value_sum + flip_pairs(value_term, level_index)
        else:
            back_key, back_value = from_partner(
                (key_term.astype(jnp.bfloat16), value_term.astype(jnp.bfloat16)),
                "seq",
                level_index - inner_bits,
            )
            grad_key_sum = grad_key_sum + back_key.astype(jnp.float32)
            grad_value_sum = grad_value_sum + back_value.astype(jnp.float32)
    key_partial = global_terms[0].astype(jnp.bfloat16).astype(jnp.float32)
    value_partial = global_terms[1].astype(jnp.bfloat16).astype(jnp.float32)
    key_share, value_share = (
        lax.psum_scatter(
            key_partial.astype(jnp.bfloat16), "seq", scatter_dimension=1, tiled=True
        ).astype(jnp.float32),
        lax.psum_scatter(
            value_partial.astype(jnp.bfloat16), "seq", scatter_dimension=1, tiled=True
        ).astype(jnp.float32),
    )
    every_block = jnp.arange(total_blocks, dtype=jnp.int32)
    route_weight = (
        (global_blocks[:, None] == every_block[None, :])
        .astype(jnp.float32)
        .T[:, :, None, None, None]
    )
    key_send = jnp.sum(route_weight * key_share[None], 1)
    value_send = jnp.sum(route_weight * value_share[None], 1)
    key_owned, value_owned = (
        lax.all_to_all(
            key_send.astype(jnp.bfloat16), "seq", split_axis=0, concat_axis=1, tiled=True
        ).astype(key_send.dtype),
        lax.all_to_all(
            value_send.astype(jnp.bfloat16), "seq", split_axis=0, concat_axis=1, tiled=True
        ).astype(value_send.dtype),
    )
    grad_key_sum = grad_key_sum + key_owned
    grad_value_sum = grad_value_sum + value_owned
    return (
        attended_groups.reshape(queries.shape),
        grad_query_groups.reshape(queries.shape),
        grad_key_sum.astype(jnp.bfloat16).reshape(queries.shape),
        grad_value_sum.astype(jnp.bfloat16).reshape(queries.shape),
    )


NT = (((1,), (1,)), ((), ()))
NN = (((1,), (0,)), ((), ()))


def product(left, right, dims):
    return lax.dot_general(left, right, dims, preferred_element_type=jnp.float32)


def head_kernel(
    level_count,
    inner_bits,
    scaling,
    seq_count,
    start,
    finish,
    source_count,
    globals_ref,
    *refs,
):
    sources, refs = refs[:source_count], refs[source_count:]
    if start == 0:
        key_parts, refs = refs[:seq_count], refs[seq_count:]
        out_ref, key_ref, value_ref, key_flip, value_flip, *refs = refs
    else:
        key_ref, value_ref, key_flip, value_flip, key_carry, value_carry, out_ref, *refs = refs
    if finish:
        total_ref, *refs = refs
    else:
        key_out, value_out, *refs = refs
    key_sum, value_sum, logit_ref, weight_ref, table_ref = refs
    step = pl.program_id(0)
    block = step + start
    total_blocks = key_flip.shape[0]
    width = key_flip.shape[1]
    inner_mask = (1 << inner_bits) - 1
    near_count = 1 + level_count
    global_count = globals_ref.shape[0]
    factor = scaling * math.log2(math.e)

    @pl.when(step == 0)
    def _():
        if start == 0:
            for place in range(seq_count):
                for inner in range(inner_mask + 1):
                    index = (place << inner_bits) + inner
                    keys, values = key_parts[place][0, inner], key_parts[place][1, inner]
                    key_ref[index] = keys
                    value_ref[index] = values
                    key_flip[index] = keys.astype(jnp.float32).T.astype(jnp.bfloat16)
                    value_flip[index] = values.astype(jnp.float32).T.astype(jnp.bfloat16)

        def prepare(index, carry):
            if start:
                key_sum[index] = key_carry[index]
                value_sum[index] = value_carry[index]
            else:
                key_sum[index] = jnp.zeros((BLOCK, width), jnp.float32)
                value_sum[index] = jnp.zeros((BLOCK, width), jnp.float32)
            return carry

        lax.fori_loop(0, total_blocks, prepare, 0)

    kept = jnp.int32(0)
    for member in range(global_count):
        target = globals_ref[member]
        offset = target ^ block
        table_ref[kept] = target
        kept = kept + ((offset & (offset - 1)) != 0).astype(jnp.int32)
    slot_total = near_count + kept
    fixed_count = near_count + max(0, global_count - near_count)

    def block_of(slot):
        if isinstance(slot, int) and slot < near_count:
            return block ^ (0 if slot == 0 else 1 << (slot - 1))
        return table_ref[slot - near_count]

    def over_slots(body, carry):
        for slot in range(fixed_count):
            carry = body(slot, carry)
        return lax.fori_loop(fixed_count, slot_total, body, carry)

    source, member = step >> inner_bits, step & inner_mask
    query, grad = sources[0][0, member], sources[0][1, member]
    for place in range(1, source_count):
        here = source == place
        query = jnp.where(here, sources[place][0, member], query)
        grad = jnp.where(here, sources[place][1, member], grad)

    def logits_step(slot, peak):
        index = block_of(slot)
        keys = key_ref[index]
        logits = product(keys, query, NT)
        logit_ref[slot] = logits
        return jnp.maximum(peak, jnp.max(logits.reshape(BLOCK // 8, 8, BLOCK), 0))

    peak = over_slots(logits_step, jnp.full((8, BLOCK), -jnp.inf, jnp.float32))
    peak = jnp.max(peak, 0, keepdims=True) * factor

    def weights_step(slot, carry):
        total, output = carry
        weights = jnp.exp2(logit_ref[slot] * factor - peak)
        total = total + jnp.sum(weights.reshape(BLOCK // 8, 8, BLOCK), 0)
        weights = weights.astype(jnp.bfloat16)
        weight_ref[slot] = weights
        return (total, output + product(value_flip[block_of(slot)], weights, NN))

    total, output = over_slots(
        weights_step,
        (jnp.zeros((8, BLOCK), jnp.float32), jnp.zeros((width, BLOCK), jnp.float32)),
    )
    inverse = 1.0 / jnp.sum(total, 0, keepdims=True)
    output = output * inverse
    grad_wide = grad.astype(jnp.float32)
    row_delta = jnp.sum(output * grad_wide.T, 0, keepdims=True)
    column = jnp.broadcast_to(inverse, (width, BLOCK)).T
    query_scaled = (query.astype(jnp.float32) * (column * scaling)).astype(jnp.bfloat16)
    grad_scaled = (grad_wide * column).astype(jnp.bfloat16)

    def backward_step(slot, grad_query):
        index = block_of(slot)
        values = value_ref[index]
        weights = weight_ref[slot]
        grad_weights = product(values, grad, NT)
        grad_logits = (weights.astype(jnp.float32) * (grad_weights - row_delta)).astype(
            jnp.bfloat16
        )
        key_sum[index] += product(grad_logits, query_scaled, NN)
        value_sum[index] += product(weights, grad_scaled, NN)
        return grad_query + product(key_flip[index], grad_logits, NN)

    grad_query = over_slots(backward_step, jnp.zeros((width, BLOCK), jnp.float32))
    grad_query = grad_query * (inverse * scaling)
    out_ref[0, 0, 0] = output.T.astype(jnp.bfloat16)
    out_ref[0, 1, 0] = grad_query.T.astype(jnp.bfloat16)

    @pl.when(step == pl.num_programs(0) - 1)
    def _():
        def hand_on(index, carry):
            if finish:
                major, minor = index >> inner_bits, index & inner_mask
                total_ref[major, 0, minor] = key_sum[index].astype(jnp.bfloat16)
                total_ref[major, 1, minor] = value_sum[index].astype(jnp.bfloat16)
            else:
                key_out[index] = key_sum[index]
                value_out[index] = value_sum[index]
            return carry

        lax.fori_loop(0, total_blocks, hand_on, 0)


def head_attention(query_parts, key_parts, global_blocks, state, seq_count, start, finish):
    part_shape = query_parts[0].shape
    _, block_count, _, width = part_shape
    total_blocks = seq_count * block_count
    level_count = total_blocks.bit_length() - 1
    inner_bits = block_count.bit_length() - 1
    slot_count = 1 + level_count + global_blocks.shape[0]
    inner_mask = block_count - 1
    steps = len(query_parts) * block_count

    def whole(shape):
        return pl.BlockSpec(
            shape, lambda step: (0,) * len(shape), pipeline_mode=pl.Buffered(1)
        )

    flip_shape = (total_blocks, width, BLOCK)
    sum_shape = (total_blocks, BLOCK, width)
    total_shape = (seq_count,) + part_shape
    in_specs = [pl.BlockSpec(memory_space=pltpu.SMEM)]
    in_specs += [whole(part_shape)] * (len(query_parts) + len(key_parts))
    out_shape = [jax.ShapeDtypeStruct((len(query_parts),) + part_shape, jnp.bfloat16)]
    out_specs = [
        pl.BlockSpec(
            (1, 2, 1, BLOCK, width), lambda step: (step >> inner_bits, 0, step & inner_mask, 0, 0)
        )
    ]
    if start == 0:
        out_shape += [jax.ShapeDtypeStruct(sum_shape, jnp.bfloat16)] * 2
        out_shape += [jax.ShapeDtypeStruct(flip_shape, jnp.bfloat16)] * 2
        out_specs += [whole(sum_shape)] * 2 + [whole(flip_shape)] * 2
    else:
        in_specs += [whole(sum_shape)] * 2 + [whole(flip_shape)] * 2 + [whole(sum_shape)] * 2
    if finish:
        out_shape += [jax.ShapeDtypeStruct(total_shape, jnp.bfloat16)]
        out_specs += [whole(total_shape)]
    else:
        out_shape += [jax.ShapeDtypeStruct(sum_shape, jnp.float32)] * 2
        out_specs += [whole(sum_shape)] * 2
    pairs = steps * slot_count * BLOCK * BLOCK
    return pl.pallas_call(
        functools.partial(
            head_kernel,
            level_count,
            inner_bits,
            1.0 / math.sqrt(width),
            seq_count,
            start * block_count,
            finish,
            len(query_parts),
        ),
        grid=(steps,),
        out_shape=out_shape,
        in_specs=in_specs,
        out_specs=out_specs,
        scratch_shapes=[
            pltpu.VMEM(sum_shape, jnp.float32),
            pltpu.VMEM(sum_shape, jnp.float32),
            pltpu.VMEM((slot_count, BLOCK, BLOCK), jnp.float32),
            pltpu.VMEM((slot_count, BLOCK, BLOCK), jnp.bfloat16),
            pltpu.SMEM((global_blocks.shape[0],), jnp.int32),
        ],
        compiler_params=pltpu.CompilerParams(
            dimension_semantics=("arbitrary",), vmem_limit_bytes=40 * 1024 * 1024
        ),
        cost_estimate=pl.CostEstimate(
            flops=48 * pairs * width, bytes_accessed=16 * total_blocks * BLOCK * width, transcendentals=pairs
        ),
    )(global_blocks, *query_parts, *key_parts, *state)


def swap(array, distance):
    pairs = [(source, source ^ distance) for source in range(lax.axis_size("seq"))]
    return lax.ppermute(array, "seq", pairs) if distance else array


def after(array, earlier):
    return lax.optimization_barrier((array, earlier))[0]


def head_plan(queries, key_rows, value_rows, grad_out, global_blocks):
    row_count, head_count, head_width = queries.shape
    seq_count = lax.axis_size("seq")
    block_count = row_count // BLOCK
    me = lax.axis_index("seq")
    pack_shape = (2, block_count, BLOCK, head_width)

    def pack(first, second):
        packed = jnp.stack([first.transpose(1, 0, 2), second.transpose(1, 0, 2)], 1)
        packed = packed.reshape((head_count,) + pack_shape)
        return [
            lax.dynamic_index_in_dim(packed, me ^ distance, 0, keepdims=False)
            for distance in range(seq_count)
        ]

    key_send = pack(key_rows, value_rows)
    query_send = pack(queries, grad_out)
    quarter = seq_count // 4
    near, far = range(1, 2 * quarter), range(2 * quarter, seq_count)
    key_parts, query_parts = [key_send[0]], [query_send[0]]
    for distance in near:
        key_parts.append(swap(after(key_send[distance], key_parts[-1]), distance))
    key_parts += [swap(key_send[distance], distance) for distance in far]
    earlier = key_parts[2 * quarter - 1]
    for distance in near:
        query_parts.append(swap(after(query_send[distance], earlier), distance))
        earlier = query_parts[-1]
    for distance in range(2 * quarter, 3 * quarter):
        query_parts.append(swap(after(query_send[distance], key_parts[distance]), distance))
    relabelled = global_blocks ^ (me * block_count)
    state = ()
    query_back = [None] * seq_count

    def attend(start, earlier, finish=False):
        parts = query_parts[start : start + quarter]
        if earlier:
            parts = [after(part, earlier) for part in parts]
        out, *rest = head_attention(
            parts, () if start else key_parts, relabelled, state, seq_count, start, finish
        )
        return out, rest

    def give_back(start, out):
        for distance in range(start, start + quarter):
            query_back[distance] = swap(out[distance - start], distance)

    out, rest = attend(0, None)
    fixed, state = tuple(rest[:4]), tuple(rest)
    give_back(0, out)
    for distance in range(3 * quarter, seq_count):
        query_parts.append(swap(after(query_send[distance], out), distance))
    out, rest = attend(2 * quarter, None)
    state = fixed + tuple(rest)
    give_back(2 * quarter, out)
    out, rest = attend(3 * quarter, query_back[1:quarter])
    state = fixed + tuple(rest)
    give_back(3 * quarter, out)
    out, (totals,) = attend(quarter, query_back[2 * quarter : 3 * quarter], True)
    last = query_back[3 * quarter :]
    key_back = [totals[0]]
    key_back += [
        swap(after(totals[distance], last), distance) for distance in range(1, seq_count)
    ]
    give_back(quarter, after(out, key_back[1 : 1 + quarter]))

    def unpack(parts):
        stacked = jnp.stack(parts, 0)
        ordered = jnp.stack(
            [
                lax.dynamic_index_in_dim(stacked, me ^ head, 0, keepdims=False)
                for head in range(head_count)
            ],
            0,
        ).reshape(head_count, 2, row_count, head_width)
        return (ordered[:, 0].transpose(1, 0, 2), ordered[:, 1].transpose(1, 0, 2))

    return unpack(query_back) + unpack(key_back)


def on_device(*operands):
    seq_count = lax.axis_size("seq")
    one_head_each = operands[0].shape[1] == seq_count and seq_count % 4 == 0
    return (head_plan if one_head_each else gathered_plan)(*operands)


def solution(mesh):
    in_specs = (
        P(("groups", "seq"), ("head", "sub"), None),
        P(("groups", "seq"), ("head", "sub"), None),
        P(("groups", "seq"), ("head", "sub"), None),
        P(("groups", "seq"), ("head", "sub"), None),
        P("groups"),
    )
    out_specs = (
        P(("groups", "seq"), ("head", "sub"), None),
        P(("groups", "seq"), ("head", "sub"), None),
        P(("groups", "seq"), ("head", "sub"), None),
        P(("groups", "seq"), ("head", "sub"), None),
    )
    return jax.shard_map(
        on_device, mesh=mesh, in_specs=in_specs, out_specs=out_specs, check_vma=False
    )
```

```python
import functools
import math

import jax
import jax.numpy as jnp
from jax import lax
from jax.experimental import pallas as pl
from jax.experimental.pallas import tpu as pltpu
from jax.sharding import PartitionSpec as P

BLOCK = 256


def shortened(array):

    def short(part):
        return part.astype(jnp.bfloat16) if part.dtype == jnp.float32 else part

    return jax.tree.map(short, array)


def from_partner(value, axis, bit):
    mask = 2**bit
    pairs = [(source, source ^ mask) for source in range(lax.axis_size(axis))]
    return lax.ppermute(value, axis, pairs)


def spread(array, axis, root):
    mine = lax.axis_index(axis) == root
    return lax.psum(jnp.where(mine, array, jnp.zeros_like(array)), axis)


def flip_pairs(array, bit_index):
    block_count = array.shape[0]
    stride = 1 << bit_index
    shaped = array.reshape((block_count // (2 * stride), 2, stride) + array.shape[1:])
    return jnp.flip(shaped, 1).reshape(array.shape)


def fetch_first(pair, bit_index):
    return jax.tree.map(
        lambda part, own: part.astype(own.dtype),
        from_partner(shortened(pair), "seq", bit_index),
        pair,
    )


def partner_stack(key_blocks, value_blocks, inner_bits, level_count, fetcher):
    key_list = [key_blocks]
    value_list = [value_blocks]
    for level_index in range(level_count):
        if level_index < inner_bits:
            key_list.append(flip_pairs(key_blocks, level_index))
            value_list.append(flip_pairs(value_blocks, level_index))
        else:
            far_keys, far_values = fetcher((key_blocks, value_blocks), level_index - inner_bits)
            key_list.append(far_keys)
            value_list.append(far_values)
    return (jnp.stack(key_list, 1), jnp.stack(value_list, 1))


def group_logits(query_group, key_group, global_keys, keep_group, scaling):
    near_part = jnp.einsum(
        "gqhd,glkhd->ghqlk", query_group, key_group, preferred_element_type=jnp.float32
    )
    far_part = jnp.einsum(
        "gqhd,nkhd->ghqnk", query_group, global_keys, preferred_element_type=jnp.float32
    )
    far_part = jnp.where(keep_group[:, None, None, :, None], far_part * scaling, -jnp.inf)
    lead_shape = near_part.shape[:3]
    return jnp.concatenate(
        [near_part.reshape(lead_shape + (-1,)) * scaling, far_part.reshape(lead_shape + (-1,))], -1
    )


def split_keys(array, slot_count, block_rows):
    lead_shape = array.shape[:3]
    near_part = array[..., : slot_count * block_rows].reshape(lead_shape + (slot_count, block_rows))
    far_part = array[..., slot_count * block_rows :].reshape(lead_shape + (-1, block_rows))
    return (near_part, far_part)


def gathered_plan(queries, key_rows, value_rows, grad_out, global_blocks):
    row_count, head_count, head_width = queries.shape
    block_count = row_count // BLOCK
    seq_count = lax.axis_size("seq")
    total_blocks = block_count * seq_count
    level_count = total_blocks.bit_length() - 1
    inner_bits = block_count.bit_length() - 1
    slot_count = 1 + level_count
    global_count = global_blocks.shape[0]
    scaling = 1.0 / math.sqrt(head_width)
    first_block = lax.axis_index("seq") * block_count
    block_shape = (block_count, BLOCK, head_count, head_width)
    query_blocks = queries.reshape(block_shape)
    key_blocks = key_rows.reshape(block_shape)
    value_blocks = value_rows.reshape(block_shape)
    grad_blocks = grad_out.reshape(block_shape)
    block_ids = first_block + jnp.arange(block_count, dtype=jnp.int32)
    xor_offsets = jnp.bitwise_xor(global_blocks[None, :], block_ids[:, None])
    keep_global = jnp.bitwise_and(xor_offsets, xor_offsets - 1) != 0
    picked_keys = []
    picked_values = []
    for member in range(global_count):
        target = global_blocks[member]
        local_index = target % block_count
        key_single = lax.dynamic_index_in_dim(key_blocks, local_index, 0, keepdims=False)
        value_single = lax.dynamic_index_in_dim(value_blocks, local_index, 0, keepdims=False)
        key_got, value_got = (
            spread(key_single, "seq", target // block_count),
            spread(value_single, "seq", target // block_count),
        )
        picked_keys.append(key_got)
        picked_values.append(value_got)
    global_keys = jnp.stack(picked_keys, 0)
    global_values = jnp.stack(picked_values, 0)
    key_stack, value_stack = partner_stack(
        key_blocks, value_blocks, inner_bits, level_count, fetch_first
    )
    pair_count = block_count // 2

    def grouped(array):
        return array.reshape((pair_count, 2) + array.shape[1:])

    def forward_group(operands):
        query_group, key_group, value_group, keep_group = operands
        logits = group_logits(query_group, key_group, global_keys, keep_group, scaling)
        row_peak = jnp.max(logits, -1, keepdims=True)
        log_total = row_peak + jnp.log(jnp.sum(jnp.exp(logits - row_peak), -1, keepdims=True))
        weights = jnp.exp(logits - log_total).astype(jnp.bfloat16)
        near_weights, far_weights = split_keys(weights, slot_count, BLOCK)
        output = jnp.einsum(
            "ghqlk,glkhd->gqhd", near_weights, value_group, preferred_element_type=jnp.float32
        )
        output = output + jnp.einsum(
            "ghqnk,nkhd->gqhd", far_weights, global_values, preferred_element_type=jnp.float32
        )
        return (output.astype(jnp.bfloat16), log_total)

    attended_groups, log_totals = lax.map(
        forward_group,
        (grouped(query_blocks), grouped(key_stack), grouped(value_stack), grouped(keep_global)),
    )

    def backward_group(carried, operands):
        key_sum_now, value_sum_now = carried
        query_group, key_group, value_group, keep_group, grad_group, output_group, total_group = (
            operands
        )
        logits = group_logits(query_group, key_group, global_keys, keep_group, scaling)
        weights = jnp.exp(logits - total_group)
        weights_low = weights.astype(jnp.bfloat16)
        row_delta = jnp.sum(
            grad_group.astype(jnp.float32) * output_group.astype(jnp.float32), -1
        ).transpose(0, 2, 1)
        near_grad = jnp.einsum(
            "gqhd,glkhd->ghqlk", grad_group, value_group, preferred_element_type=jnp.float32
        )
        far_grad = jnp.einsum(
            "gqhd,nkhd->ghqnk", grad_group, global_values, preferred_element_type=jnp.float32
        )
        lead_shape = near_grad.shape[:3]
        grad_weights = jnp.concatenate(
            [near_grad.reshape(lead_shape + (-1,)), far_grad.reshape(lead_shape + (-1,))], -1
        )
        grad_logits = (weights * (grad_weights - row_delta[..., None]) * scaling).astype(
            jnp.bfloat16
        )
        near_logit, far_logit = split_keys(grad_logits, slot_count, BLOCK)
        near_weight, far_weight = split_keys(weights_low, slot_count, BLOCK)
        grad_query = jnp.einsum(
            "ghqlk,glkhd->gqhd", near_logit, key_group, preferred_element_type=jnp.float32
        )
        grad_query = grad_query + jnp.einsum(
            "ghqnk,nkhd->gqhd", far_logit, global_keys, preferred_element_type=jnp.float32
        )
        key_terms = jnp.einsum(
            "ghqlk,gqhd->glkhd", near_logit, query_group, preferred_element_type=jnp.float32
        )
        value_terms = jnp.einsum(
            "ghqlk,gqhd->glkhd", near_weight, grad_group, preferred_element_type=jnp.float32
        )
        key_sum_now = key_sum_now + jnp.einsum(
            "ghqnk,gqhd->nkhd", far_logit, query_group, preferred_element_type=jnp.float32
        )
        value_sum_now = value_sum_now + jnp.einsum(
            "ghqnk,gqhd->nkhd", far_weight, grad_group, preferred_element_type=jnp.float32
        )
        return (
            (key_sum_now, value_sum_now),
            (grad_query.astype(jnp.bfloat16), key_terms, value_terms),
        )

    global_zeros = jnp.zeros((global_count, BLOCK, head_count, head_width), jnp.float32)
    global_terms, back_outputs = lax.scan(
        backward_group,
        (global_zeros, global_zeros),
        (
            grouped(query_blocks),
            grouped(key_stack),
            grouped(value_stack),
            grouped(keep_global),
            grouped(grad_blocks),
            attended_groups,
            log_totals,
        ),
    )
    grad_query_groups, key_term_groups, value_term_groups = back_outputs
    slot_shape = (block_count, slot_count, BLOCK, head_count, head_width)
    key_terms_all = key_term_groups.reshape(slot_shape)
    value_terms_all = value_term_groups.reshape(slot_shape)
    grad_key_sum = key_terms_all[:, 0]
    grad_value_sum = value_terms_all[:, 0]
    for level_index in range(level_count):
        key_term = key_terms_all[:, 1 + level_index]
        value_term = value_terms_all[:, 1 + level_index]
        if level_index < inner_bits:
            grad_key_sum = grad_key_sum + flip_pairs(key_term, level_index)
            grad_value_sum = grad_value_sum + flip_pairs(value_term, level_index)
        else:
            back_key, back_value = from_partner(
                (key_term.astype(jnp.bfloat16), value_term.astype(jnp.bfloat16)),
                "seq",
                level_index - inner_bits,
            )
            grad_key_sum = grad_key_sum + back_key.astype(jnp.float32)
            grad_value_sum = grad_value_sum + back_value.astype(jnp.float32)
    key_partial = global_terms[0].astype(jnp.bfloat16).astype(jnp.float32)
    value_partial = global_terms[1].astype(jnp.bfloat16).astype(jnp.float32)
    key_share, value_share = (
        lax.psum_scatter(
            key_partial.astype(jnp.bfloat16), "seq", scatter_dimension=1, tiled=True
        ).astype(jnp.float32),
        lax.psum_scatter(
            value_partial.astype(jnp.bfloat16), "seq", scatter_dimension=1, tiled=True
        ).astype(jnp.float32),
    )
    every_block = jnp.arange(total_blocks, dtype=jnp.int32)
    route_weight = (
        (global_blocks[:, None] == every_block[None, :])
        .astype(jnp.float32)
        .T[:, :, None, None, None]
    )
    key_send = jnp.sum(route_weight * key_share[None], 1)
    value_send = jnp.sum(route_weight * value_share[None], 1)
    key_owned, value_owned = (
        lax.all_to_all(
            key_send.astype(jnp.bfloat16), "seq", split_axis=0, concat_axis=1, tiled=True
        ).astype(key_send.dtype),
        lax.all_to_all(
            value_send.astype(jnp.bfloat16), "seq", split_axis=0, concat_axis=1, tiled=True
        ).astype(value_send.dtype),
    )
    grad_key_sum = grad_key_sum + key_owned
    grad_value_sum = grad_value_sum + value_owned
    return (
        attended_groups.reshape(queries.shape),
        grad_query_groups.reshape(queries.shape),
        grad_key_sum.astype(jnp.bfloat16).reshape(queries.shape),
        grad_value_sum.astype(jnp.bfloat16).reshape(queries.shape),
    )


NT = (((1,), (1,)), ((), ()))
NN = (((1,), (0,)), ((), ()))


def product(left, right, dims):
    return lax.dot_general(left, right, dims, preferred_element_type=jnp.float32)


def head_kernel(
    level_count,
    inner_bits,
    scaling,
    seq_count,
    start,
    finish,
    source_count,
    globals_ref,
    *refs,
):
    sources, refs = refs[:source_count], refs[source_count:]
    if start == 0:
        key_parts, refs = refs[:seq_count], refs[seq_count:]
        out_ref, key_ref, value_ref, key_flip, value_flip, *refs = refs
    else:
        key_ref, value_ref, key_flip, value_flip, key_carry, value_carry, out_ref, *refs = refs
    if finish:
        total_ref, *refs = refs
    else:
        key_out, value_out, *refs = refs
    key_sum, value_sum, logit_ref, weight_ref, table_ref = refs
    step = pl.program_id(0)
    block = step + start
    total_blocks = key_flip.shape[0]
    width = key_flip.shape[1]
    inner_mask = (1 << inner_bits) - 1
    near_count = 1 + level_count
    global_count = globals_ref.shape[0]
    factor = scaling * math.log2(math.e)

    @pl.when(step == 0)
    def _():
        if start == 0:
            for place in range(seq_count):
                for inner in range(inner_mask + 1):
                    index = (place << inner_bits) + inner
                    keys, values = key_parts[place][0, inner], key_parts[place][1, inner]
                    key_ref[index] = keys
                    value_ref[index] = values
                    key_flip[index] = keys.astype(jnp.float32).T.astype(jnp.bfloat16)
                    value_flip[index] = values.astype(jnp.float32).T.astype(jnp.bfloat16)

        def prepare(index, carry):
            if start:
                key_sum[index] = key_carry[index]
                value_sum[index] = value_carry[index]
            else:
                key_sum[index] = jnp.zeros((BLOCK, width), jnp.float32)
                value_sum[index] = jnp.zeros((BLOCK, width), jnp.float32)
            return carry

        lax.fori_loop(0, total_blocks, prepare, 0)

    kept = jnp.int32(0)
    for member in range(global_count):
        target = globals_ref[member]
        offset = target ^ block
        table_ref[kept] = target
        kept = kept + ((offset & (offset - 1)) != 0).astype(jnp.int32)
    slot_total = near_count + kept
    fixed_count = near_count + max(0, global_count - near_count)

    def block_of(slot):
        if isinstance(slot, int) and slot < near_count:
            return block ^ (0 if slot == 0 else 1 << (slot - 1))
        return table_ref[slot - near_count]

    def over_slots(body, carry):
        for slot in range(fixed_count):
            carry = body(slot, carry)
        return lax.fori_loop(fixed_count, slot_total, body, carry)

    source, member = step >> inner_bits, step & inner_mask
    query, grad = sources[0][0, member], sources[0][1, member]
    for place in range(1, source_count):
        here = source == place
        query = jnp.where(here, sources[place][0, member], query)
        grad = jnp.where(here, sources[place][1, member], grad)

    def logits_step(slot, peak):
        index = block_of(slot)
        keys = key_ref[index]
        logits = product(keys, query, NT)
        logit_ref[slot] = logits
        return jnp.maximum(peak, jnp.max(logits.reshape(BLOCK // 8, 8, BLOCK), 0))

    peak = over_slots(logits_step, jnp.full((8, BLOCK), -jnp.inf, jnp.float32))
    peak = jnp.max(peak, 0, keepdims=True) * factor

    def weights_step(slot, carry):
        total, output = carry
        weights = jnp.exp2(logit_ref[slot] * factor - peak)
        total = total + jnp.sum(weights.reshape(BLOCK // 8, 8, BLOCK), 0)
        weights = weights.astype(jnp.bfloat16)
        weight_ref[slot] = weights
        return (total, output + product(value_flip[block_of(slot)], weights, NN))

    total, output = over_slots(
        weights_step,
        (jnp.zeros((8, BLOCK), jnp.float32), jnp.zeros((width, BLOCK), jnp.float32)),
    )
    inverse = 1.0 / jnp.sum(total, 0, keepdims=True)
    output = output * inverse
    grad_wide = grad.astype(jnp.float32)
    row_delta = jnp.sum(output * grad_wide.T, 0, keepdims=True)
    column = jnp.broadcast_to(inverse, (width, BLOCK)).T
    query_scaled = (query.astype(jnp.float32) * (column * scaling)).astype(jnp.bfloat16)
    grad_scaled = (grad_wide * column).astype(jnp.bfloat16)

    def backward_step(slot, grad_query):
        index = block_of(slot)
        values = value_ref[index]
        weights = weight_ref[slot]
        grad_weights = product(values, grad, NT)
        grad_logits = (weights.astype(jnp.float32) * (grad_weights - row_delta)).astype(
            jnp.bfloat16
        )
        key_sum[index] += product(grad_logits, query_scaled, NN)
        value_sum[index] += product(weights, grad_scaled, NN)
        return grad_query + product(key_flip[index], grad_logits, NN)

    grad_query = over_slots(backward_step, jnp.zeros((width, BLOCK), jnp.float32))
    grad_query = grad_query * (inverse * scaling)
    out_ref[0, 0, 0] = output.T.astype(jnp.bfloat16)
    out_ref[0, 1, 0] = grad_query.T.astype(jnp.bfloat16)

    @pl.when(step == pl.num_programs(0) - 1)
    def _():
        def hand_on(index, carry):
            if finish:
                major, minor = index >> inner_bits, index & inner_mask
                total_ref[major, 0, minor] = key_sum[index].astype(jnp.bfloat16)
                total_ref[major, 1, minor] = value_sum[index].astype(jnp.bfloat16)
            else:
                key_out[index] = key_sum[index]
                value_out[index] = value_sum[index]
            return carry

        lax.fori_loop(0, total_blocks, hand_on, 0)


def head_attention(query_parts, key_parts, global_blocks, state, seq_count, start, finish):
    part_shape = query_parts[0].shape
    _, block_count, _, width = part_shape
    total_blocks = seq_count * block_count
    level_count = total_blocks.bit_length() - 1
    inner_bits = block_count.bit_length() - 1
    slot_count = 1 + level_count + global_blocks.shape[0]
    inner_mask = block_count - 1
    steps = len(query_parts) * block_count

    def whole(shape):
        return pl.BlockSpec(
            shape, lambda step: (0,) * len(shape), pipeline_mode=pl.Buffered(1)
        )

    flip_shape = (total_blocks, width, BLOCK)
    sum_shape = (total_blocks, BLOCK, width)
    total_shape = (seq_count,) + part_shape
    in_specs = [pl.BlockSpec(memory_space=pltpu.SMEM)]
    in_specs += [whole(part_shape)] * (len(query_parts) + len(key_parts))
    out_shape = [jax.ShapeDtypeStruct((len(query_parts),) + part_shape, jnp.bfloat16)]
    out_specs = [
        pl.BlockSpec(
            (1, 2, 1, BLOCK, width), lambda step: (step >> inner_bits, 0, step & inner_mask, 0, 0)
        )
    ]
    if start == 0:
        out_shape += [jax.ShapeDtypeStruct(sum_shape, jnp.bfloat16)] * 2
        out_shape += [jax.ShapeDtypeStruct(flip_shape, jnp.bfloat16)] * 2
        out_specs += [whole(sum_shape)] * 2 + [whole(flip_shape)] * 2
    else:
        in_specs += [whole(sum_shape)] * 2 + [whole(flip_shape)] * 2 + [whole(sum_shape)] * 2
    if finish:
        out_shape += [jax.ShapeDtypeStruct(total_shape, jnp.bfloat16)]
        out_specs += [whole(total_shape)]
    else:
        out_shape += [jax.ShapeDtypeStruct(sum_shape, jnp.float32)] * 2
        out_specs += [whole(sum_shape)] * 2
    pairs = steps * slot_count * BLOCK * BLOCK
    return pl.pallas_call(
        functools.partial(
            head_kernel,
            level_count,
            inner_bits,
            1.0 / math.sqrt(width),
            seq_count,
            start * block_count,
            finish,
            len(query_parts),
        ),
        grid=(steps,),
        out_shape=out_shape,
        in_specs=in_specs,
        out_specs=out_specs,
        scratch_shapes=[
            pltpu.VMEM(sum_shape, jnp.float32),
            pltpu.VMEM(sum_shape, jnp.float32),
            pltpu.VMEM((slot_count, BLOCK, BLOCK), jnp.float32),
            pltpu.VMEM((slot_count, BLOCK, BLOCK), jnp.bfloat16),
            pltpu.SMEM((global_blocks.shape[0],), jnp.int32),
        ],
        compiler_params=pltpu.CompilerParams(
            dimension_semantics=("arbitrary",), vmem_limit_bytes=40 * 1024 * 1024
        ),
        cost_estimate=pl.CostEstimate(
            flops=48 * pairs * width, bytes_accessed=16 * total_blocks * BLOCK * width, transcendentals=pairs
        ),
    )(global_blocks, *query_parts, *key_parts, *state)


def swap(array, distance):
    pairs = [(source, source ^ distance) for source in range(lax.axis_size("seq"))]
    return lax.ppermute(array, "seq", pairs) if distance else array


def after(array, earlier):
    return lax.optimization_barrier((array, earlier))[0]


def head_plan(queries, key_rows, value_rows, grad_out, global_blocks):
    row_count, head_count, head_width = queries.shape
    seq_count = lax.axis_size("seq")
    block_count = row_count // BLOCK
    me = lax.axis_index("seq")
    pack_shape = (2, block_count, BLOCK, head_width)

    def pack(first, second):
        packed = jnp.stack([first.transpose(1, 0, 2), second.transpose(1, 0, 2)], 1)
        packed = packed.reshape((head_count,) + pack_shape)
        return [
            lax.dynamic_index_in_dim(packed, me ^ distance, 0, keepdims=False)
            for distance in range(seq_count)
        ]

    key_send = pack(key_rows, value_rows)
    query_send = pack(queries, grad_out)
    quarter = seq_count // 4
    near, far = range(1, 2 * quarter), range(2 * quarter, seq_count)
    key_parts, query_parts = [key_send[0]], query_send[:1] + [None] * (seq_count - 1)
    for distance in range(1, seq_count):
        part = key_send[distance]
        if distance in near and distance > 1:
            part = after(part, key_parts[1])
        key_parts.append(swap(part, distance))
    for distance in [*range(1, quarter), *range(2 * quarter, 3 * quarter)]:
        earlier = key_parts[1]
        if distance in far:
            earlier = [key_parts[distance], key_parts[distance + quarter]]
        query_parts[distance] = swap(after(query_send[distance], earlier), distance)
    for distance in range(quarter, 2 * quarter):
        query_parts[distance] = swap(
            after(query_send[distance], query_parts[max(distance - 1, 1)]), distance
        )
    relabelled = global_blocks ^ (me * block_count)
    state = ()
    query_back = [None] * seq_count

    def attend(start, earlier, finish=False):
        parts = query_parts[start : start + quarter]
        if earlier:
            parts = [after(part, earlier) for part in parts]
        out, *rest = head_attention(
            parts, () if start else key_parts, relabelled, state, seq_count, start, finish
        )
        return out, rest

    def give_back(start, out):
        for distance in range(start, start + quarter):
            query_back[distance] = swap(out[distance - start], distance)

    out, rest = attend(0, None)
    fixed, state = tuple(rest[:4]), tuple(rest)
    give_back(0, out)
    for distance in range(3 * quarter, seq_count):
        query_parts[distance] = swap(after(query_send[distance], out), distance)
    out, rest = attend(2 * quarter, None)
    state = fixed + tuple(rest)
    give_back(2 * quarter, out)
    out, rest = attend(3 * quarter, query_back[1:quarter])
    state = fixed + tuple(rest)
    give_back(3 * quarter, out)
    out, (totals,) = attend(quarter, query_back[2 * quarter : 3 * quarter], True)
    last = query_back[3 * quarter :]
    key_back = [totals[0]]
    key_back += [
        swap(after(totals[distance], last), distance) for distance in range(1, seq_count)
    ]
    give_back(quarter, after(out, key_back[1 : 1 + quarter]))

    def unpack(parts):
        stacked = jnp.stack(parts, 0)
        ordered = jnp.stack(
            [
                lax.dynamic_index_in_dim(stacked, me ^ head, 0, keepdims=False)
                for head in range(head_count)
            ],
            0,
        ).reshape(head_count, 2, row_count, head_width)
        return (ordered[:, 0].transpose(1, 0, 2), ordered[:, 1].transpose(1, 0, 2))

    return unpack(query_back) + unpack(key_back)


def on_device(*operands):
    seq_count = lax.axis_size("seq")
    one_head_each = operands[0].shape[1] == seq_count and seq_count % 4 == 0
    return (head_plan if one_head_each else gathered_plan)(*operands)


def solution(mesh):
    in_specs = (
        P(("groups", "seq"), ("head", "sub"), None),
        P(("groups", "seq"), ("head", "sub"), None),
        P(("groups", "seq"), ("head", "sub"), None),
        P(("groups", "seq"), ("head", "sub"), None),
        P("groups"),
    )
    out_specs = (
        P(("groups", "seq"), ("head", "sub"), None),
        P(("groups", "seq"), ("head", "sub"), None),
        P(("groups", "seq"), ("head", "sub"), None),
        P(("groups", "seq"), ("head", "sub"), None),
    )
    return jax.shard_map(
        on_device, mesh=mesh, in_specs=in_specs, out_specs=out_specs, check_vma=False
    )
```
